32 devices in a mesh: ctx: 8 (over z, core), tp: 4 (over y, x).
Axes of the slice: x: 2, y: 2, z: 4, core: 2. Of those that a mesh axis runs over, the one named last changes fastest.
Arguments:
- tokens: bfloat16 [2048, 4096], P('ctx', 'tp'), may hold values from -6 to 6
- w_z: bfloat16 [4096, 2048], P(None, 'tp'), may hold values from -0.09375 to 0.09375
- w_x: bfloat16 [4096, 2048], P(None, 'tp'), may hold values from -0.09375 to 0.09375
- w_bc: bfloat16 [4096, 512], P(None, 'tp'), may hold values from -0.09375 to 0.09375
- conv_x: float32 [4, 2048], P(None, 'tp'), may hold values from -3 to 3
- conv_bc: float32 [4, 512], P(None, 'tp'), may hold values from -3 to 3
- bias_x: float32 [2048], P('tp'), may hold values from -0.5 to 0.5
- bias_bc: float32 [512], P('tp'), may hold values from -0.5 to 0.5
- decay_logarithm: float32 [2048, 32], P('ctx', 'tp'), may hold values from -1.3 to 0, as said below
- head_step: float32 [32], P('tp'), may hold values from 0 to 0.3, as said below
- skip: float32 [32], P('tp'), may hold values from 0.5 to 1.5
- gain: float32 [2048], P('tp'), may hold values from 0.5 to 1.5
Outputs:
- normed: bfloat16 [2048, 2048], P('ctx', 'tp')
The draws below stay inside these ranges and needn't reach their ends.
Inputs may be any that keep to these rules, and one draw needn't show every extreme that they name: decay_logarithm is negative. head_step is positive.
All inputs are finite; a program needn't handle non-finite values.
Results may differ from the reference program's by a relative error of at most 0.0095.
Values may be sent and summed in bfloat16 or wider, within the bound.
No kernel may reach another device: no remote copies, remote signals or barrier semaphores. Data moves between devices by JAX's collectives and lax.ppermute only.
A program may use at most 64 MiB of HBM per device.

```python
import jax
import jax.numpy as jnp
from jax import lax

D = 4096
P_SIZE = 64
N = 128
KERNEL = 4
STRETCH = 256
TOK_DEV = 256
HEADS = 32
GROUP_HEADS = 16
GROUPS = 2
D_INNER = 2048
TOKENS = 2048


def head_rates(key):
    base_key = jax.random.fold_in(key, 11)
    pick_key, slow_key, quick_key = jax.random.split(base_key, 3)
    fast_share = 0.5
    quick_heads = jax.random.bernoulli(pick_key, fast_share, (HEADS,))
    slow_rate = jnp.exp(jax.random.uniform(slow_key, (HEADS,), jnp.float32, jnp.log(0.05), jnp.log(0.5))) / TOKENS
    quick_rate = jnp.exp(jax.random.uniform(quick_key, (HEADS,), jnp.float32, jnp.log(1.0 / 50.0), jnp.log(1.0 / 30.0)))
    return jnp.where(quick_heads, quick_rate, slow_rate)


def draw_head_step(key, part):
    rates = head_rates(key)
    return (1.5 * jnp.sqrt(rates)).astype(jnp.float32)


def draw_decay_logarithm(key, part):
    rates = head_rates(key)
    own_key = jax.random.fold_in(key, 23)
    block_key, token_key, place_key, loss_key = jax.random.split(own_key, 4)
    block_total = TOKENS // TOK_DEV
    block_factor = jnp.exp(jax.random.uniform(block_key, (block_total, HEADS), jnp.float32, jnp.log(0.5), jnp.log(2.0)))
    token_factor = jnp.exp(jax.random.uniform(token_key, (TOKENS, HEADS), jnp.float32, jnp.log(0.7), jnp.log(1.4)))
    factor = jnp.repeat(block_factor, TOK_DEV, axis=0) * token_factor
    constant_rate = -rates[None, :] * factor
    token_places = jax.random.randint(place_key, (2, HEADS), 0, TOKENS)
    error_values = jax.random.uniform(loss_key, (2, HEADS), jnp.float32, 0.2, 0.45)
    token_positions = jnp.arange(TOKENS)[:, None]
    token_runs = jnp.where(token_positions == token_places[0][None, :], jnp.log1p(-error_values[0])[None, :], 0.0)
    token_runs = token_runs + jnp.where(token_positions == token_places[1][None, :], jnp.log1p(-error_values[1])[None, :], 0.0)
    return (constant_rate + token_runs).astype(jnp.float32)


def block_levels(rng, dims, cuts, least, largest):
    factor_of = 1.0
    for position, parts in cuts:
        draws = jax.random.uniform(jax.random.fold_in(jax.random.fold_in(rng, 6), position), (parts,), jnp.float32, least / len(cuts), largest / len(cuts))
        factor_of = factor_of * jnp.repeat(jnp.exp(draws), dims[position] // parts).reshape((-1,) + (1,) * (len(dims) - 1 - position))
    return factor_of


def centred(key, dims, scale, most, shards=(), kind=jnp.bfloat16):
    factor_of = block_levels(key, dims, shards, -0.22, 0.18) if shards else 1.0
    drawn = jax.random.normal(key, dims, jnp.float32) * scale * factor_of
    return jnp.minimum(jnp.maximum(drawn, -most), most).astype(kind)


def setup_inputs(seed: int = 0) -> dict:
    seeds = jax.random.split(jax.random.key(seed), 13)
    tokens = centred(seeds[0], (TOKENS, D), 1.0, 6.0, ((0, 8), (1, 4)))
    w_z = centred(seeds[1], (D, D_INNER), D ** -0.5, 0.09375, ((1, 4),))
    w_x = centred(seeds[2], (D, D_INNER), D ** -0.5, 0.09375, ((1, 4),))
    w_bc = centred(seeds[3], (D, 2 * GROUPS * N), D ** -0.5, 0.09375, ((1, 4),))
    conv_x = centred(seeds[4], (KERNEL, D_INNER), KERNEL ** -0.5, 3.0, ((1, 4),), jnp.float32)
    conv_bc = centred(seeds[5], (KERNEL, 2 * GROUPS * N), KERNEL ** -0.5, 3.0, ((1, 4),), jnp.float32)
    bias_x = jnp.clip(jax.random.uniform(seeds[6], (D_INNER,), jnp.float32, -0.5, 0.5) * block_levels(seeds[6], (D_INNER,), ((0, 4),), -0.4, 0.0), -0.5, 0.5)
    bias_bc = jnp.clip(jax.random.uniform(seeds[7], (2 * GROUPS * N,), jnp.float32, -0.5, 0.5) * block_levels(seeds[7], (2 * GROUPS * N,), ((0, 4),), -0.4, 0.0), -0.5, 0.5)
    decay_logarithm = draw_decay_logarithm(jax.random.fold_in(seeds[12], 71), 0)
    head_step = draw_head_step(jax.random.fold_in(seeds[12], 71), 0)
    skip = jnp.clip(0.5 + 1.0 * jax.random.uniform(seeds[10], (HEADS,), jnp.float32) ** block_levels(seeds[10], (HEADS,), ((0, 4),), -0.2, 0.2), 0.5, 1.5)
    gain = jnp.clip(1.0 + 0.1 * jax.random.normal(seeds[11], (D_INNER,), jnp.float32), 0.5, 1.5)
    return dict(tokens=tokens, w_z=w_z, w_x=w_x, w_bc=w_bc, conv_x=conv_x, conv_bc=conv_bc, bias_x=bias_x, bias_bc=bias_bc, decay_logarithm=decay_logarithm, head_step=head_step, skip=skip, gain=gain)


def causal_conv(pre_conv, taps, offset_bias):
    width = pre_conv.shape[1]
    extended = jnp.concatenate([jnp.zeros((KERNEL - 1, width), jnp.float32), pre_conv.astype(jnp.float32)], axis=0)
    total = offset_bias[None, :] + jnp.zeros((TOKENS, width), jnp.float32)
    for offset in range(KERNEL):
        total = total + taps[offset][None, :] * extended[offset:offset + TOKENS]
    return jax.nn.silu(total).astype(jnp.bfloat16)

def group_scan(inputs):
    x_group, decay_group, b_group, c_group, step_group = inputs
    stretch_count = TOKENS // STRETCH
    x_blocks = x_group.astype(jnp.float32).reshape(stretch_count, STRETCH, GROUP_HEADS, P_SIZE)
    decay_blocks = decay_group.reshape(stretch_count, STRETCH, GROUP_HEADS)
    b_blocks = b_group.astype(jnp.float32).reshape(stretch_count, STRETCH, N)
    c_blocks = c_group.astype(jnp.float32).reshape(stretch_count, STRETCH, N)
    causal = jnp.tril(jnp.ones((STRETCH, STRETCH), dtype=bool))[:, :, None]

    def one_block(state, block):
        x_block, decay_block, b_block, c_block = block
        cum_decay = jnp.cumsum(decay_block, axis=0)
        pair_diff = cum_decay[:, None, :] - cum_decay[None, :, :]
        segment = jnp.where(causal, jnp.exp(jnp.where(causal, pair_diff, 0.0)), 0.0)
        scores = jnp.dot(c_block, b_block.T, precision=lax.Precision.HIGHEST)
        mixing = segment * scores[:, :, None] * step_group
        intra_out = jnp.einsum('ijh,jhp->ihp', mixing, x_block, precision=lax.Precision.HIGHEST)
        inter_out = jnp.einsum('in,hpn->ihp', c_block, state, precision=lax.Precision.HIGHEST) * jnp.exp(cum_decay)[:, :, None]
        end_weight = jnp.exp(cum_decay[-1][None, :] - cum_decay) * step_group
        added = jnp.einsum('jh,jhp,jn->hpn', end_weight, x_block, b_block, precision=lax.Precision.HIGHEST)
        new_state = jnp.exp(cum_decay[-1])[:, None, None] * state + added
        return (new_state, intra_out + inter_out)
    start_state = jnp.zeros((GROUP_HEADS, P_SIZE, N), jnp.float32)
    _, outputs = lax.scan(one_block, start_state, (x_blocks, decay_blocks, b_blocks, c_blocks))
    return outputs.reshape(TOKENS, GROUP_HEADS, P_SIZE)

def reference(tokens, w_z, w_x, w_bc, conv_x, conv_bc, bias_x, bias_bc, decay_logarithm, head_step, skip, gain):
    gate_in = jnp.dot(tokens, w_z, preferred_element_type=jnp.float32).astype(jnp.bfloat16)
    x_pre = jnp.dot(tokens, w_x, preferred_element_type=jnp.float32).astype(jnp.bfloat16)
    bc_pre = jnp.dot(tokens, w_bc, preferred_element_type=jnp.float32).astype(jnp.bfloat16)
    x_conv = causal_conv(x_pre, conv_x, bias_x)
    bc_conv = causal_conv(bc_pre, conv_bc, bias_bc).reshape(TOKENS, GROUPS, 2, N)
    b_all = jnp.transpose(bc_conv[:, :, 0, :], (1, 0, 2))
    c_all = jnp.transpose(bc_conv[:, :, 1, :], (1, 0, 2))
    x_groups = jnp.transpose(x_conv.reshape(TOKENS, GROUPS, GROUP_HEADS, P_SIZE), (1, 0, 2, 3))
    decay_groups = jnp.transpose(decay_logarithm.reshape(TOKENS, GROUPS, GROUP_HEADS), (1, 0, 2))
    step_groups = head_step.reshape(GROUPS, GROUP_HEADS)
    scanned = lax.map(group_scan, (x_groups, decay_groups, b_all, c_all, step_groups))
    scanned = jnp.transpose(scanned, (1, 0, 2, 3)).reshape(TOKENS, HEADS, P_SIZE)
    head_out = scanned + skip[None, :, None] * x_conv.astype(jnp.float32).reshape(TOKENS, HEADS, P_SIZE)
    gated = head_out.reshape(TOKENS, D_INNER) * jax.nn.silu(gate_in.astype(jnp.float32))
    grouped = gated.reshape(TOKENS, GROUPS, GROUP_HEADS * P_SIZE)
    mean_square = lax.optimization_barrier(jnp.mean(grouped * grouped, axis=2))
    scaled = grouped * lax.rsqrt(mean_square + 1e-05)[:, :, None]
    return (scaled.reshape(TOKENS, D_INNER) * gain[None, :]).astype(jnp.bfloat16)
```

```python
import jax
import jax.numpy as jnp
from jax import lax
from jax.sharding import PartitionSpec as P

KERNEL = 4
STRETCH = 256
RIM = 8


def hop(value, axis, distance):
    size = lax.axis_size(axis)
    return lax.ppermute(value, axis, [(i, (i + distance) % size) for i in range(size)])


def onward(value, axis, distance):
    size = lax.axis_size(axis)
    route = [(i, i + distance) for i in range(size) if i + distance < size]
    return lax.ppermute(value, axis, route)


def partner(value, axis, mask):
    pairs = [(i, i ^ mask) for i in range(lax.axis_size(axis))]
    return lax.ppermute(value, axis, pairs)


def gathered_blocks(tokens, axis):
    size = lax.axis_size(axis)
    half = tokens.shape[0] // 2
    first, second = tokens[:half], tokens[half:]
    blocks = [(0, tokens)]
    if size == 1:
        return blocks
    near_1 = partner(first, axis, 1)
    if size == 2:
        near_2 = partner(second, axis, 1)
        return blocks + [(1, jnp.concatenate([near_1, near_2], 0))]
    far_2 = partner(second, axis, 2)
    near_2 = partner(second, axis, 1)
    far_1 = partner(first, axis, 2)
    across_1 = partner(near_1, axis, 2)
    across_2 = partner(far_2, axis, 1)
    blocks.append((1, jnp.concatenate([near_1, near_2], 0)))
    blocks.append((2, jnp.concatenate([far_1, far_2], 0)))
    blocks.append((3, jnp.concatenate([across_1, across_2], 0)))
    mask = 4
    while mask < size:
        blocks += [(m | mask, partner(b, axis, mask)) for m, b in blocks]
        mask *= 2
    return blocks


def gathered_rim(rows, axis):
    size, place = lax.axis_size(axis), lax.axis_index(axis)
    rows = rows[None]
    mask = 1
    while mask < size:
        other = partner(rows, axis, mask)
        high = (place // mask) % 2 == 1
        rows = jnp.concatenate(
            [jnp.where(high, other, rows), jnp.where(high, rows, other)], axis=0
        )
        mask *= 2
    return rows.transpose(1, 0, 2).reshape(rows.shape[1], -1)


def causal_conv(rim, body, taps, bias):
    rows = body.shape[0]
    extended = jnp.concatenate([rim[RIM - KERNEL + 1 :], body], axis=0).astype(jnp.float32)
    total = bias[None, :]
    for offset in range(KERNEL):
        total = total + taps[offset][None, :] * extended[offset : offset + rows]
    return jax.nn.silu(total).astype(jnp.bfloat16)


def local(
    tokens, w_z, w_x, w_bc, conv_x, conv_bc, bias_x, bias_bc, decay_logarithm, head_step, skip, gain
):
    f32, bf16 = jnp.float32, jnp.bfloat16
    rows, depth = tokens.shape
    width = w_x.shape[1]
    heads = head_step.shape[0]
    dim = width // heads
    n = w_bc.shape[1]
    tp_place = lax.axis_index("tp")
    ctx_size, ctx_place = lax.axis_size("ctx"), lax.axis_index("ctx")
    chips, chip, core = ctx_size // 2, ctx_place // 2, ctx_place % 2

    rim_tokens = gathered_rim(onward(tokens[rows - RIM :], "ctx", 1), "tp")

    cum = jnp.cumsum(decay_logarithm, axis=0)
    total = cum[-1]
    total_sibling = partner(total, "ctx", 1)
    total_chip = total + total_sibling
    chip_before = [hop(total_chip, "ctx", 2 * k) for k in range(1, chips - 1)]

    def product(block, weights):
        return jnp.dot(block, weights, preferred_element_type=f32)

    def projected(blocks, weights):
        acc = None
        for mask, block in blocks:
            part = lax.dynamic_slice_in_dim(weights, (tp_place ^ mask) * depth, depth, 0)
            term = product(block, part)
            acc = term if acc is None else acc + term
        return acc.astype(bf16)

    blocks = gathered_blocks(tokens, "tp")
    bc_rim = product(rim_tokens, w_bc).astype(bf16)
    x_rim = product(rim_tokens, w_x).astype(bf16)
    bc_pre = projected(blocks, w_bc)
    own_bc = causal_conv(bc_rim, bc_pre, conv_bc, bias_bc)
    other_bc = partner(own_bc, "tp", 1)
    x_pre = projected(blocks, w_x)
    x_conv = causal_conv(x_rim, x_pre, conv_x, bias_x)
    holds_b = tp_place % 2 == 0
    b_proj = jnp.where(holds_b, own_bc, other_bc)
    c_proj = jnp.where(holds_b, other_bc, own_bc)

    x_heads = x_conv.reshape(rows, heads, dim)
    end_weight = jnp.exp(total[None, :] - cum) * head_step
    weighted = (x_heads.astype(f32) * end_weight[:, :, None]).astype(bf16)
    state = lax.dot_general(
        weighted.reshape(rows, width), b_proj, (((0,), (0,)), ((), ())), preferred_element_type=f32
    )
    state = state.reshape(2, width // 2, n)

    def rows_of(per_head):
        return jnp.repeat(per_head.reshape(2, heads // 2), dim, axis=1)

    def mine(halves):
        return jnp.where(core == 0, halves[0], halves[1])

    def others(halves):
        return jnp.where(core == 0, halves[1], halves[0])

    kept = mine(state)
    sibling = partner(others(state).astype(bf16), "ctx", 1).astype(f32)
    first_state = jnp.where(core == 0, kept, sibling)
    second_state = jnp.where(core == 0, sibling, kept)
    first_decay = jnp.where(core == 0, total, total_sibling)
    second_decay = jnp.where(core == 0, total_sibling, total)
    chip_state = second_state + jnp.exp(mine(rows_of(second_decay)))[:, None] * first_state
    send = chip_state.astype(bf16)
    before = jnp.zeros_like(chip_state)
    between = jnp.zeros_like(total)
    for k in range(1, chips):
        got = hop(send, "ctx", 2 * k).astype(f32)
        weight = jnp.where(chip >= k, jnp.exp(mine(rows_of(between))), 0.0)
        before = before + weight[:, None] * got
        if k < chips - 1:
            between = between + jnp.where(chip >= k, chip_before[k - 1], 0.0)
    after_first = first_state + jnp.exp(mine(rows_of(first_decay)))[:, None] * before
    keep = jnp.where(core == 0, before, after_first).astype(bf16)
    give = jnp.where(core == 0, after_first, before).astype(bf16)
    take = partner(give, "ctx", 1)
    low = jnp.where(core == 0, keep, take)
    high = jnp.where(core == 0, take, keep)
    entering = jnp.concatenate([low, high], axis=0)

    scores = lax.dot_general(
        c_proj, b_proj, (((1,), (1,)), ((), ())), preferred_element_type=f32
    )
    causal = jnp.tril(jnp.ones((rows, rows), dtype=bool))[None]
    cum_heads = cum.T
    pair_diff = cum_heads[:, :, None] - cum_heads[:, None, :]
    segment = jnp.where(causal, jnp.exp(jnp.where(causal, pair_diff, 0.0)), 0.0)
    mixing = (segment * scores[None] * head_step[:, None, None]).astype(bf16)
    intra = jnp.einsum("hij,jhp->ihp", mixing, x_heads, preferred_element_type=f32)
    intra = intra + skip[None, :, None] * x_heads.astype(f32)
    gate = jax.nn.silu(projected(blocks, w_z).astype(f32))

    inter = lax.dot_general(
        c_proj, entering, (((1,), (1,)), ((), ())), preferred_element_type=f32
    ).reshape(rows, heads, dim)
    out = intra + inter * jnp.exp(cum)[:, :, None]
    gated = out.reshape(rows, width) * gate
    local_square = jnp.sum(gated * gated, axis=1)
    other_square = partner(local_square, "tp", 1)
    mean_square = (local_square + other_square) / (2 * width)
    scaled = gated * lax.rsqrt(mean_square + 1e-05)[:, None]
    return (scaled * gain[None, :]).astype(bf16)


def solution(mesh):
    in_specs = (
        P("ctx", "tp"),
        P(None, "tp"),
        P(None, "tp"),
        P(None, "tp"),
        P(None, "tp"),
        P(None, "tp"),
        P("tp"),
        P("tp"),
        P("ctx", "tp"),
        P("tp"),
        P("tp"),
        P("tp"),
    )
    out_specs = P("ctx", "tp")
    return jax.shard_map(local, mesh=mesh, in_specs=in_specs, out_specs=out_specs, check_vma=False)
```

```python
import functools

import jax
import jax.numpy as jnp
from jax import lax
from jax.experimental import pallas as pl
from jax.experimental.pallas import tpu as pltpu
from jax.sharding import PartitionSpec as P

KERNEL = 4
RIM = 8
PAD = 8
F32, BF16 = jnp.float32, jnp.bfloat16
EXACT = lax.Precision.HIGHEST
VMEM = pl.BlockSpec(memory_space=pltpu.VMEM)
HBM = pl.BlockSpec(memory_space=pltpu.HBM)


def run(body, outs, *operands, scratch=(), flops=1000000, hbm=0, limit=4 << 20):
    single = not isinstance(outs, list)
    shapes = [jax.ShapeDtypeStruct(*o) for o in ([outs] if single else outs)]
    results = pl.pallas_call(
        body,
        out_shape=shapes,
        in_specs=[HBM] * hbm + [VMEM] * (len(operands) - hbm),
        out_specs=[VMEM] * len(shapes),
        scratch_shapes=list(scratch),
        compiler_params=pltpu.CompilerParams(vmem_limit_bytes=limit),
        cost_estimate=pl.CostEstimate(flops=flops, bytes_accessed=flops // 400, transcendentals=0),
        name=body.func.__name__ if isinstance(body, functools.partial) else body.__name__,
    )(*operands)
    return results[0] if single else results


def hop(value, axis, distance):
    size = lax.axis_size(axis)
    return lax.ppermute(value, axis, [(i, (i + distance) % size) for i in range(size)])


def partner(value, axis, mask):
    return lax.ppermute(value, axis, [(i, i ^ mask) for i in range(lax.axis_size(axis))])


def dot(a, b, **kwargs):
    return jnp.dot(a, b, preferred_element_type=F32, **kwargs)


def silu(v):
    return v / (1.0 + jnp.exp(-v))


def holds_b():
    return lax.axis_index("tp") % 2 == 0


def first_core():
    return lax.axis_index("ctx") % 2 == 0


def fetched_rows(start, source, out, arrival):
    copy = pltpu.make_async_copy(source.at[pl.ds(start, out.shape[0])], out, arrival)
    copy.start()
    copy.wait()


def own_product(w_bc, w_x, w_z, top, bottom, sums, weights, arrivals):
    size, depth, _ = weights.shape
    place = lax.axis_index("tp")
    copies = []
    for mask in range(size):
        source_rows = pl.ds(pl.multiple_of(jnp.bitwise_xor(place, mask) * depth, depth), depth)
        column = 0
        for i, w in enumerate((w_bc, w_x, w_z)):
            columns = pl.ds(column, w.shape[1])
            copies.append(
                pltpu.make_async_copy(
                    w.at[source_rows], weights.at[mask, :, columns], arrivals.at[mask, i]
                )
            )
            column += w.shape[1]
    for copy in copies:
        copy.start()
    for copy in copies[:3]:
        copy.wait()
    sums[...] = dot(jnp.concatenate([top[...], bottom[...]], axis=0), weights[0])
    for copy in copies[3:]:
        copy.wait()


def block_of(pieces, i):
    return jnp.concatenate([pieces[2 * i][...], pieces[2 * i + 1][...]], axis=0)


def middle_product(masks, *refs):
    pieces, (weights, before, _, out) = refs[: 2 * len(masks)], refs[2 * len(masks) :]
    total = before[...]
    for i, mask in enumerate(masks):
        total += dot(block_of(pieces, i), weights[mask])
    out[...] = total


def rim_product(rim, weights, out):
    total = None
    for mask in range(weights.shape[0]):
        columns = pl.ds(0, out.shape[1])
        term = dot(rim[pl.ds(mask * RIM, RIM), :], weights[mask, :, columns])
        total = term if total is None else total + term
    inside = lax.axis_index("ctx") > 0
    out[...] = jnp.where(inside, total, 0.0).astype(BF16).astype(F32)


def finished(masks, pieces, weights, before, start, width):
    columns = pl.ds(start, width)
    total = before[:, columns]
    for i, mask in enumerate(masks):
        total += dot(block_of(pieces, i), weights[mask, :, columns])
    return total.astype(BF16).astype(F32)


def convolved(pre, rim, taps, bias, extended):
    rows = pre.shape[0]
    extended[pl.ds(0, RIM), :] = rim
    extended[pl.ds(RIM, rows), :] = pre
    total = bias[...]
    for k in range(KERNEL):
        total = total + taps[pl.ds(k, 1), :] * extended[pl.ds(RIM - KERNEL + 1 + k, rows), :]
    return silu(total).astype(BF16)


def last_bc(masks, *refs):
    pieces, refs = refs[: 2 * len(masks)], refs[2 * len(masks) :]
    weights, before, rim, taps, bias, out, extended = refs
    width = out.shape[1]
    pre = finished(masks, pieces, weights, before, 0, width)
    out[...] = convolved(pre, rim[:, pl.ds(0, width)], taps, bias, extended)


def last_x(masks, *refs):
    pieces, refs = refs[: 2 * len(masks)], refs[2 * len(masks) :]
    weights, before, rim, taps, bias, end_weight, x_out, weighted_out, extended = refs
    width = x_out.shape[1]
    start = rim.shape[1] - width
    pre = finished(masks, pieces, weights, before, start, width)
    x = convolved(pre, rim[:, pl.ds(start, width)], taps, bias, extended)
    x_out[...] = x
    weighted_out[...] = (x.astype(F32) * end_weight[...]).astype(BF16)


def last_z(masks, *refs):
    pieces, (weights, before, _, out) = refs[: 2 * len(masks)], refs[2 * len(masks) :]
    width = out.shape[1]
    out[...] = silu(finished(masks, pieces, weights, before, before.shape[1] - width, width))


def decays(decay_t, step, skip, segment, grown, end_weight, whole, skip_wide):
    heads, rows = decay_t.shape
    width = grown.shape[1]
    dim = width // heads
    spread = (
        lax.broadcasted_iota(jnp.int32, (heads, width), 1) // dim
        == lax.broadcasted_iota(jnp.int32, (heads, width), 0)
    ).astype(F32)
    i = lax.broadcasted_iota(jnp.int32, (rows, rows), 0)
    j = lax.broadcasted_iota(jnp.int32, (rows, rows), 1)
    causal = i >= j
    cum = lax.dot_general(
        causal.astype(F32),
        decay_t[...],
        (((1,), (1,)), ((), ())),
        precision=EXACT,
        preferred_element_type=F32,
    )
    cum_t = dot(decay_t[...], (i <= j).astype(F32), precision=EXACT)
    cum_wide = dot(cum, spread, precision=EXACT)
    total = cum_wide[rows - 1 :]
    grown[...] = jnp.exp(cum_wide)
    end_weight[...] = jnp.exp(total - cum_wide) * dot(step[...], spread, precision=EXACT)
    whole[...] = jnp.broadcast_to(jnp.exp(total), whole.shape)
    skip_wide[...] = dot(skip[...], spread, precision=EXACT)
    for h in range(heads):
        difference = cum[:, h : h + 1] - cum_t[h : h + 1, :]
        factor = jnp.where(causal, jnp.exp(jnp.where(causal, difference, 0.0)), 0.0)
        segment[h] = (factor * step[:, h : h + 1]).astype(BF16)


def halves(wide):
    half = wide.shape[1] // 2
    return wide[:, :half], wide[:, half:]


def mine_other(wide):
    low, high = halves(wide)
    first = first_core()
    return jnp.where(first, low, high), jnp.where(first, high, low)


def write_message(out, state, decay):
    n = state.shape[0]
    out[pl.ds(0, n), :] = state.astype(BF16)
    decay = jnp.broadcast_to(decay, (PAD, decay.shape[1]))
    high = decay.astype(BF16).astype(F32)
    out[pl.ds(n, 2 * PAD), :] = jnp.concatenate([high, decay - high], axis=0).astype(BF16)


def read_message(ref):
    n = ref.shape[0] - 2 * PAD
    tail = ref[pl.ds(n, 2 * PAD), :].astype(F32)
    return ref[pl.ds(0, n), :].astype(F32), tail[:1] + tail[PAD : PAD + 1]


def section_state(own_bc, other_bc, weighted, whole, message, kept):
    b = jnp.where(holds_b(), own_bc[...], other_bc[...])
    state = lax.dot_general(
        b, weighted[...], (((0,), (0,)), ((), ())), preferred_element_type=F32
    )
    mine, other = mine_other(state)
    _, other_decay = mine_other(whole[...])
    kept[...] = mine
    write_message(message, other, other_decay[:1])


def pair_states(kept, whole, received):
    sibling, sibling_decay = read_message(received)
    mine_decay, _ = mine_other(whole[...])
    mine_decay = mine_decay[:1]
    first = first_core()
    mine = kept[...]
    return (
        (jnp.where(first, mine, sibling), jnp.where(first, mine_decay, sibling_decay)),
        (jnp.where(first, sibling, mine), jnp.where(first, sibling_decay, mine_decay)),
    )


def chip_state(kept, whole, received, message):
    (first, first_decay), (second, second_decay) = pair_states(kept, whole, received)
    write_message(message, second + second_decay * first, first_decay * second_decay)


def entering_state(kept, whole, received, *refs):
    got, (_, _, keep, give) = refs[:-4], refs[-4:]
    (first, first_decay), _ = pair_states(kept, whole, received)
    chip = lax.axis_index("ctx") // 2
    before = jnp.zeros_like(first)
    between = jnp.ones_like(first_decay)
    for k, ref in enumerate(got):
        state, decay = read_message(ref)
        before += jnp.where(chip > k, between, 0.0) * state
        between = between * decay
    after = first + first_decay * before
    lead = first_core()
    keep[...] = jnp.where(lead, before, after).astype(BF16)
    give[...] = jnp.where(lead, after, before).astype(BF16)


def within_section(own_bc, other_bc, x, segment, skip_wide, _, out):
    own, other = own_bc[...], other_bc[...]
    b = jnp.where(holds_b(), own, other)
    c = jnp.where(holds_b(), other, own)
    scores = lax.dot_general(c, b, (((1,), (1,)), ((), ())), preferred_element_type=F32)
    heads = segment.shape[0]
    dim = x.shape[1] // heads
    low = lax.broadcasted_iota(jnp.int32, (1, 2 * dim), 1) < dim
    for pair in range(heads // 2):
        columns = pl.ds(pair * 2 * dim, 2 * dim)
        mixing = jnp.concatenate(
            [(segment[2 * pair + s].astype(F32) * scores).astype(BF16) for s in range(2)], axis=1
        )
        both = x[:, columns]
        wide = both.astype(F32)
        stacked = jnp.concatenate(
            [jnp.where(low, wide, 0.0).astype(BF16), jnp.where(low, 0.0, wide).astype(BF16)], axis=0
        )
        out[:, columns] = dot(mixing, stacked) + skip_wide[:, columns] * wide


def gated_output(own_bc, other_bc, keep, take, within, grown, gate, gated_out, square_out):
    lead = first_core()
    low = jnp.where(lead, keep[...], take[...])
    high = jnp.where(lead, take[...], keep[...])
    c = jnp.where(holds_b(), other_bc[...], own_bc[...])
    half = low.shape[1]
    squares = None
    for s, entering in enumerate((low, high)):
        columns = pl.ds(s * half, half)
        inter = dot(c, entering) * grown[:, columns]
        gated = (within[:, columns] + inter) * gate[:, columns]
        gated_out[:, columns] = gated
        for start in range(0, half, 128):
            part = gated[:, start : start + 128]
            squares = part * part if squares is None else squares + part * part
    ones = jnp.ones((PAD, squares.shape[1]), F32)
    square_out[...] = lax.dot_general(
        ones, squares, (((1,), (1,)), ((), ())), precision=EXACT, preferred_element_type=F32
    )


def normed_output(gated, square, other_square, gain, out):
    width = gated.shape[1]
    mean = (square[...] + other_square[...]) / (2 * width)
    factor = lax.rsqrt(mean + 1e-05)
    share = jnp.full((PAD, 128), 1.0 / PAD, F32)
    column = lax.dot_general(
        factor, share, (((0,), (0,)), ((), ())), precision=EXACT, preferred_element_type=F32
    )
    for start in range(0, width, 128):
        columns = pl.ds(start, 128)
        out[:, columns] = (gated[:, columns] * column * gain[:, columns]).astype(BF16)


def gather_pieces(top, bottom, axis):
    size = lax.axis_size(axis)
    end = bottom.shape[0] - RIM
    near_bottom = partner(bottom, axis, 1)
    rim = jnp.concatenate([bottom[end:], near_bottom[end:]], axis=0)
    if size == 2:
        return {}, {1: [partner(top, axis, 1), near_bottom]}, rim
    far_top = partner(top, axis, 2)
    near_top = partner(top, axis, 1)
    far_bottom = partner(bottom, axis, 2)
    rim = jnp.concatenate([rim, partner(rim, axis, 2)], axis=0)
    across_bottom = partner(near_bottom, axis, 2)
    across_top = partner(far_top, axis, 1)
    early = {1: [near_top, near_bottom], 2: [far_top, far_bottom]}
    last = {3: [across_top, across_bottom]}
    mask = 4
    while mask < size:
        early = {**early, **last}
        last = {m | mask: [partner(h, axis, mask) for h in p] for m, p in early.items()}
        last[mask] = [partner(h, axis, mask) for h in (top, bottom)]
        rim = jnp.concatenate([rim, partner(rim, axis, mask)], axis=0)
        mask *= 2
    return early, last, rim


def local(
    tokens, w_z, w_x, w_bc, conv_x, conv_bc, bias_x, bias_bc, decay_logarithm, head_step, skip, gain
):
    rows, depth = tokens.shape
    width, bc_width = w_x.shape[1], w_bc.shape[1]
    heads = head_step.shape[0]
    n = bc_width
    chips = lax.axis_size("ctx") // 2

    half = rows // 2
    arrival = [pltpu.SemaphoreType.DMA]
    bottom, top = [
        run(functools.partial(fetched_rows, start), ((half, depth), BF16), tokens, scratch=arrival, hbm=1)
        for start in (half, 0)
    ]
    early, last, rim = gather_pieces(top, bottom, "tp")
    rim = hop(rim, "ctx", 1)

    def flops(*sizes):
        total = 2
        for s in sizes:
            total *= s
        return total

    size = lax.axis_size("tp")
    everything = bc_width + 2 * width
    sums, weights = run(
        own_product,
        [((rows, everything), F32), ((size, depth, everything), BF16)],
        w_bc, w_x, w_z, top, bottom,
        scratch=[pltpu.SemaphoreType.DMA((size, 3))],
        flops=flops(rows, depth, everything),
        hbm=3,
    )
    segment, grown, end_weight, whole, skip_wide = run(
        decays,
        [
            ((heads, rows, rows), BF16),
            ((rows, width), F32),
            ((rows, width), F32),
            ((PAD, width), F32),
            ((1, width), F32),
        ],
        decay_logarithm.T, head_step.reshape(1, -1), skip.reshape(1, -1),
        flops=flops(rows, rows, width),
    )
    if early:
        masks = tuple(sorted(early))
        sums = run(
            functools.partial(middle_product, masks),
            ((rows, everything), F32),
            *[h for m in masks for h in early[m]], weights, sums, skip_wide,
            flops=len(masks) * flops(rows, depth, everything),
        )
    rim_sums = run(
        rim_product,
        ((RIM, bc_width + width), F32),
        rim, weights,
        flops=flops(rows, depth, width),
    )

    masks = tuple(sorted(last))
    ends = [h for m in masks for h in last[m]]
    own_bc = run(
        functools.partial(last_bc, masks),
        ((rows, bc_width), BF16),
        *ends, weights, sums, rim_sums, conv_bc, bias_bc.reshape(1, -1),
        scratch=[pltpu.VMEM((rows + RIM, bc_width), F32)],
        flops=flops(rows, depth, bc_width),
    )
    other_bc = partner(own_bc, "tp", 1)
    x, weighted = run(
        functools.partial(last_x, masks),
        [((rows, width), BF16), ((rows, width), BF16)],
        *ends, weights, sums, rim_sums, conv_x, bias_x.reshape(1, -1), end_weight,
        scratch=[pltpu.VMEM((rows + RIM, width), F32)],
        flops=flops(rows, depth, width),
    )
    message_shape = ((n + 2 * PAD, width // 2), BF16)
    state_shape = (n, width // 2)
    message, kept = run(
        section_state,
        [message_shape, (state_shape, F32)],
        own_bc, other_bc, weighted, whole,
        flops=flops(rows, n, width),
    )
    received = partner(message, "ctx", 1)
    message = run(chip_state, message_shape, kept, whole, received)
    got = [hop(message, "ctx", 2 * k) for k in range(1, chips)]
    within = run(
        within_section,
        ((rows, width), F32),
        own_bc, other_bc, x, segment, skip_wide, message,
        flops=3 * flops(rows, rows, width),
    )
    gate = run(
        functools.partial(last_z, masks),
        ((rows, width), F32),
        *ends, weights, sums, message,
        flops=flops(rows, depth, width),
    )
    keep, give = run(
        entering_state, [(state_shape, BF16), (state_shape, BF16)], kept, whole, received, *got, within, gate
    )
    take = partner(give, "ctx", 1)
    gated, square = run(
        gated_output,
        [((rows, width), F32), ((PAD, rows), F32)],
        own_bc, other_bc, keep, take, within, grown, gate,
        flops=flops(rows, n, width),
    )
    other_square = partner(square, "tp", 1)
    return run(
        normed_output, ((rows, width), BF16), gated, square, other_square, gain.reshape(1, -1)
    )


def solution(mesh):
    in_specs = (
        P("ctx", "tp"),
        P(None, "tp"),
        P(None, "tp"),
        P(None, "tp"),
        P(None, "tp"),
        P(None, "tp"),
        P("tp"),
        P("tp"),
        P("ctx", "tp"),
        P("tp"),
        P("tp"),
        P("tp"),
    )
    out_specs = P("ctx", "tp")
    return jax.shard_map(local, mesh=mesh, in_specs=in_specs, out_specs=out_specs, check_vma=False)
```

```python
import functools

import jax
import jax.numpy as jnp
from jax import lax
from jax.experimental import pallas as pl
from jax.experimental.pallas import tpu as pltpu
from jax.sharding import PartitionSpec as P

KERNEL = 4
RIM = 8
ROWS = 8
PAD = 4
F32, BF16 = jnp.float32, jnp.bfloat16
EXACT = lax.Precision.HIGHEST
VMEM = pl.BlockSpec(memory_space=pltpu.VMEM)
HBM = pl.BlockSpec(memory_space=pltpu.HBM)


def run(body, outs, *operands, scratch=(), flops=1000000, hbm=0, limit=4 << 20):
    single = not isinstance(outs, list)
    shapes = [jax.ShapeDtypeStruct(*o) for o in ([outs] if single else outs)]
    operands = [
        pltpu.with_memory_space_constraint(o, pltpu.HBM) if i < hbm else o
        for i, o in enumerate(operands)
    ]
    results = pl.pallas_call(
        body,
        out_shape=shapes,
        in_specs=[HBM] * hbm + [VMEM] * (len(operands) - hbm),
        out_specs=[VMEM] * len(shapes),
        scratch_shapes=list(scratch),
        compiler_params=pltpu.CompilerParams(vmem_limit_bytes=limit),
        cost_estimate=pl.CostEstimate(flops=flops, bytes_accessed=flops // 400, transcendentals=0),
        name=body.func.__name__ if isinstance(body, functools.partial) else body.__name__,
    )(*operands)
    return results[0] if single else results


def hop(value, axis, distance):
    size = lax.axis_size(axis)
    return lax.ppermute(value, axis, [(i, (i + distance) % size) for i in range(size)])


def partner(value, axis, mask):
    return lax.ppermute(value, axis, [(i, i ^ mask) for i in range(lax.axis_size(axis))])


def dot(a, b, **kwargs):
    return jnp.dot(a, b, preferred_element_type=F32, **kwargs)


def silu(v):
    return v / (1.0 + jnp.exp(-v))


def holds_b():
    return lax.axis_index("tp") % 2 == 0


def first_core():
    return lax.axis_index("ctx") % 2 == 0


def fetched_rows(start, source, out, arrival):
    copy = pltpu.make_async_copy(source.at[pl.ds(start, out.shape[0])], out, arrival)
    copy.start()
    copy.wait()


def own_product(w_bc, w_x, w_z, top, bottom, sums, weights, arrivals):
    size, depth, _ = weights.shape
    place = lax.axis_index("tp")
    copies = []
    for mask in range(size):
        source_rows = pl.ds(pl.multiple_of(jnp.bitwise_xor(place, mask) * depth, depth), depth)
        column = 0
        for i, w in enumerate((w_bc, w_x, w_z)):
            columns = pl.ds(column, w.shape[1])
            copies.append(
                pltpu.make_async_copy(
                    w.at[source_rows], weights.at[mask, :, columns], arrivals.at[mask, i]
                )
            )
            column += w.shape[1]
    for copy in copies:
        copy.start()
    for copy in copies[:3]:
        copy.wait()
    sums[...] = dot(jnp.concatenate([top[...], bottom[...]], axis=0), weights[0])
    for copy in copies[3:]:
        copy.wait()


def block_of(pieces, i):
    return jnp.concatenate([pieces[2 * i][...], pieces[2 * i + 1][...]], axis=0)


def middle_product(masks, *refs):
    pieces, (weights, before, _, out) = refs[: 2 * len(masks)], refs[2 * len(masks) :]
    total = before[...]
    for i, mask in enumerate(masks):
        total += dot(block_of(pieces, i), weights[mask])
    out[...] = total


def rim_product(rim, weights, out):
    total = None
    for mask in range(weights.shape[0]):
        columns = pl.ds(0, out.shape[1])
        term = dot(rim[pl.ds(mask * RIM, RIM), :], weights[mask, :, columns])
        total = term if total is None else total + term
    inside = lax.axis_index("ctx") > 0
    out[...] = jnp.where(inside, total, 0.0).astype(BF16).astype(F32)


def finished(masks, pieces, weights, before, start, width):
    columns = pl.ds(start, width)
    total = before[:, columns]
    for i, mask in enumerate(masks):
        total += dot(block_of(pieces, i), weights[mask, :, columns])
    return total.astype(BF16).astype(F32)


def convolved(pre, rim, taps, bias, extended):
    rows = pre.shape[0]
    extended[pl.ds(0, RIM), :] = rim
    extended[pl.ds(RIM, rows), :] = pre
    total = bias[...]
    for k in range(KERNEL):
        total = total + taps[pl.ds(k, 1), :] * extended[pl.ds(RIM - KERNEL + 1 + k, rows), :]
    return silu(total).astype(BF16)


def last_bc(masks, *refs):
    pieces, refs = refs[: 2 * len(masks)], refs[2 * len(masks) :]
    weights, before, rim, taps, bias, out, extended = refs
    width = out.shape[1]
    pre = finished(masks, pieces, weights, before, 0, width)
    out[...] = convolved(pre, rim[:, pl.ds(0, width)], taps, bias, extended)


def last_x(masks, *refs):
    pieces, refs = refs[: 2 * len(masks)], refs[2 * len(masks) :]
    weights, before, rim, taps, bias, end_weight, x_out, weighted_out, extended = refs
    width = x_out.shape[1]
    start = rim.shape[1] - width
    pre = finished(masks, pieces, weights, before, start, width)
    x = convolved(pre, rim[:, pl.ds(start, width)], taps, bias, extended)
    x_out[...] = x
    weighted_out[...] = (x.astype(F32) * end_weight[...]).astype(BF16)


def last_z(masks, *refs):
    pieces, (weights, before, _, out) = refs[: 2 * len(masks)], refs[2 * len(masks) :]
    width = out.shape[1]
    out[...] = silu(finished(masks, pieces, weights, before, before.shape[1] - width, width))


def decays(decay_t, step, skip, segment, grown, end_weight, whole, skip_wide):
    heads, rows = decay_t.shape
    width = grown.shape[1]
    dim = width // heads
    spread = (
        lax.broadcasted_iota(jnp.int32, (heads, width), 1) // dim
        == lax.broadcasted_iota(jnp.int32, (heads, width), 0)
    ).astype(F32)
    i = lax.broadcasted_iota(jnp.int32, (rows, rows), 0)
    j = lax.broadcasted_iota(jnp.int32, (rows, rows), 1)
    causal = i >= j
    cum = lax.dot_general(
        causal.astype(F32),
        decay_t[...],
        (((1,), (1,)), ((), ())),
        precision=EXACT,
        preferred_element_type=F32,
    )
    cum_t = dot(decay_t[...], (i <= j).astype(F32), precision=EXACT)
    cum_wide = dot(cum, spread, precision=EXACT)
    total = cum_wide[rows - 1 :]
    grown[...] = jnp.exp(cum_wide)
    end_weight[...] = jnp.exp(total - cum_wide) * dot(step[...], spread, precision=EXACT)
    whole[...] = jnp.broadcast_to(jnp.exp(total), whole.shape)
    skip_wide[...] = dot(skip[...], spread, precision=EXACT)
    for h in range(heads):
        difference = cum[:, h : h + 1] - cum_t[h : h + 1, :]
        factor = jnp.where(causal, jnp.exp(jnp.where(causal, difference, 0.0)), 0.0)
        segment[h] = (factor * step[:, h : h + 1]).astype(BF16)


def halves(wide):
    half = wide.shape[1] // 2
    return wide[:, :half], wide[:, half:]


def mine_other(wide):
    low, high = halves(wide)
    first = first_core()
    return jnp.where(first, low, high), jnp.where(first, high, low)


def write_message(out, state, decay):
    n = state.shape[0]
    out[pl.ds(0, n), :] = state.astype(BF16)
    decay = jnp.broadcast_to(decay, (PAD, decay.shape[1]))
    high = decay.astype(BF16).astype(F32)
    out[pl.ds(n, 2 * PAD), :] = jnp.concatenate([high, decay - high], axis=0).astype(BF16)


def read_message(ref):
    n = ref.shape[0] - 2 * PAD
    tail = ref[pl.ds(n, 2 * PAD), :].astype(F32)
    return ref[pl.ds(0, n), :].astype(F32), tail[:1] + tail[PAD : PAD + 1]


def section_state(own_bc, other_bc, weighted, whole, message, kept):
    b = jnp.where(holds_b(), own_bc[...], other_bc[...])
    state = lax.dot_general(
        b, weighted[...], (((0,), (0,)), ((), ())), preferred_element_type=F32
    )
    mine, other = mine_other(state)
    _, other_decay = mine_other(whole[...])
    kept[...] = mine
    write_message(message, other, other_decay[:1])


def pair_states(kept, whole, received):
    sibling, sibling_decay = read_message(received)
    mine_decay, _ = mine_other(whole[...])
    mine_decay = mine_decay[:1]
    first = first_core()
    mine = kept[...]
    return (
        (jnp.where(first, mine, sibling), jnp.where(first, mine_decay, sibling_decay)),
        (jnp.where(first, sibling, mine), jnp.where(first, sibling_decay, mine_decay)),
    )


def chip_state(kept, whole, received, message):
    (first, first_decay), (second, second_decay) = pair_states(kept, whole, received)
    write_message(message, second + second_decay * first, first_decay * second_decay)


def entering_state(kept, whole, received, *refs):
    got, (_, _, keep, give) = refs[:-4], refs[-4:]
    (first, first_decay), _ = pair_states(kept, whole, received)
    chip = lax.axis_index("ctx") // 2
    before = jnp.zeros_like(first)
    between = jnp.ones_like(first_decay)
    for k, ref in enumerate(got):
        state, decay = read_message(ref)
        before += jnp.where(chip > k, between, 0.0) * state
        between = between * decay
    after = first + first_decay * before
    lead = first_core()
    keep[...] = jnp.where(lead, before, after).astype(BF16)
    give[...] = jnp.where(lead, after, before).astype(BF16)


def within_section(own_bc, other_bc, x, segment, skip_wide, _, out):
    own, other = own_bc[...], other_bc[...]
    b = jnp.where(holds_b(), own, other)
    c = jnp.where(holds_b(), other, own)
    scores = lax.dot_general(c, b, (((1,), (1,)), ((), ())), preferred_element_type=F32)
    heads = segment.shape[0]
    dim = x.shape[1] // heads
    low = lax.broadcasted_iota(jnp.int32, (1, 2 * dim), 1) < dim
    for pair in range(heads // 2):
        columns = pl.ds(pair * 2 * dim, 2 * dim)
        mixing = jnp.concatenate(
            [(segment[2 * pair + s].astype(F32) * scores).astype(BF16) for s in range(2)], axis=1
        )
        both = x[:, columns]
        wide = both.astype(F32)
        stacked = jnp.concatenate(
            [jnp.where(low, wide, 0.0).astype(BF16), jnp.where(low, 0.0, wide).astype(BF16)], axis=0
        )
        out[:, columns] = dot(mixing, stacked) + skip_wide[:, columns] * wide


def gated_output(own_bc, other_bc, keep, take, within, grown, gate, gated_out, square_out):
    lead = first_core()
    low = jnp.where(lead, keep[...], take[...])
    high = jnp.where(lead, take[...], keep[...])
    c = jnp.where(holds_b(), other_bc[...], own_bc[...])
    half = low.shape[1]
    squares = None
    for s, entering in enumerate((low, high)):
        columns = pl.ds(s * half, half)
        inter = dot(c, entering) * grown[:, columns]
        gated = (within[:, columns] + inter) * gate[:, columns]
        gated_out[:, columns] = gated
        for start in range(0, half, 128):
            part = gated[:, start : start + 128]
            squares = part * part if squares is None else squares + part * part
    ones = jnp.ones((ROWS, squares.shape[1]), F32)
    square_out[...] = lax.dot_general(
        ones, squares, (((1,), (1,)), ((), ())), precision=EXACT, preferred_element_type=F32
    )


def normed_output(gated, square, other_square, gain, out):
    width = gated.shape[1]
    mean = (square[...] + other_square[...]) / (2 * width)
    factor = lax.rsqrt(mean + 1e-05)
    share = jnp.full((ROWS, 128), 1.0 / ROWS, F32)
    column = lax.dot_general(
        factor, share, (((0,), (0,)), ((), ())), precision=EXACT, preferred_element_type=F32
    )
    for start in range(0, width, 128):
        columns = pl.ds(start, 128)
        out[:, columns] = (gated[:, columns] * column * gain[:, columns]).astype(BF16)


def last_rows(bottom, near_bottom, _, out):
    end = bottom.shape[0] - RIM
    out[pl.ds(0, RIM), :] = bottom[pl.ds(end, RIM), :]
    out[pl.ds(RIM, RIM), :] = near_bottom[pl.ds(end, RIM), :]


def gather_pieces(top, bottom, sums, axis):
    size = lax.axis_size(axis)
    near_bottom = partner(bottom, axis, 1)
    rim = run(last_rows, ((2 * RIM, bottom.shape[1]), BF16), bottom, near_bottom, sums)
    if size == 2:
        return {}, {1: [partner(top, axis, 1), near_bottom]}, rim
    far_top = partner(top, axis, 2)
    near_top = partner(top, axis, 1)
    far_bottom = partner(bottom, axis, 2)
    rim = jnp.concatenate([rim, partner(rim, axis, 2)], axis=0)
    across_bottom = partner(near_bottom, axis, 2)
    across_top = partner(far_top, axis, 1)
    early = {1: [near_top, near_bottom], 2: [far_top, far_bottom]}
    last = {3: [across_top, across_bottom]}
    mask = 4
    while mask < size:
        early = {**early, **last}
        last = {m | mask: [partner(h, axis, mask) for h in p] for m, p in early.items()}
        last[mask] = [partner(h, axis, mask) for h in (top, bottom)]
        rim = jnp.concatenate([rim, partner(rim, axis, mask)], axis=0)
        mask *= 2
    return early, last, rim


def local(
    tokens, w_z, w_x, w_bc, conv_x, conv_bc, bias_x, bias_bc, decay_logarithm, head_step, skip, gain
):
    rows, depth = tokens.shape
    width, bc_width = w_x.shape[1], w_bc.shape[1]
    heads = head_step.shape[0]
    n = bc_width
    chips = lax.axis_size("ctx") // 2

    half = rows // 2
    arrival = [pltpu.SemaphoreType.DMA]
    bottom, top = [
        run(functools.partial(fetched_rows, start), ((half, depth), BF16), tokens, scratch=arrival, hbm=1)
        for start in (half, 0)
    ]
    def flops(*sizes):
        total = 2
        for s in sizes:
            total *= s
        return total

    size = lax.axis_size("tp")
    everything = bc_width + 2 * width
    sums, weights = run(
        own_product,
        [((rows, everything), F32), ((size, depth, everything), BF16)],
        w_bc, w_x, w_z, top, bottom,
        scratch=[pltpu.SemaphoreType.DMA((size, 3))],
        flops=flops(rows, depth, everything),
        hbm=3,
    )
    early, last, rim = gather_pieces(top, bottom, sums, "tp")
    rim = hop(rim, "ctx", 1)
    segment, grown, end_weight, whole, skip_wide = run(
        decays,
        [
            ((heads, rows, rows), BF16),
            ((rows, width), F32),
            ((rows, width), F32),
            ((ROWS, width), F32),
            ((1, width), F32),
        ],
        decay_logarithm.T, head_step.reshape(1, -1), skip.reshape(1, -1),
        flops=flops(rows, rows, width),
    )
    if early:
        masks = tuple(sorted(early))
        sums = run(
            functools.partial(middle_product, masks),
            ((rows, everything), F32),
            *[h for m in masks for h in early[m]], weights, sums, skip_wide,
            flops=len(masks) * flops(rows, depth, everything),
        )
    rim_sums = run(
        rim_product,
        ((RIM, bc_width + width), F32),
        rim, weights,
        flops=flops(rows, depth, width),
    )

    masks = tuple(sorted(last))
    ends = [h for m in masks for h in last[m]]
    own_bc = run(
        functools.partial(last_bc, masks),
        ((rows, bc_width), BF16),
        *ends, weights, sums, rim_sums, conv_bc, bias_bc.reshape(1, -1),
        scratch=[pltpu.VMEM((rows + RIM, bc_width), F32)],
        flops=flops(rows, depth, bc_width),
    )
    other_bc = partner(own_bc, "tp", 1)
    x, weighted = run(
        functools.partial(last_x, masks),
        [((rows, width), BF16), ((rows, width), BF16)],
        *ends, weights, sums, rim_sums, conv_x, bias_x.reshape(1, -1), end_weight,
        scratch=[pltpu.VMEM((rows + RIM, width), F32)],
        flops=flops(rows, depth, width),
    )
    message_shape = ((n + 2 * PAD, width // 2), BF16)
    state_shape = (n, width // 2)
    message, kept = run(
        section_state,
        [message_shape, (state_shape, F32)],
        own_bc, other_bc, weighted, whole,
        flops=flops(rows, n, width),
    )
    received = partner(message, "ctx", 1)
    message = run(chip_state, message_shape, kept, whole, received)
    got = [hop(message, "ctx", 2 * k) for k in range(1, chips)]
    within = run(
        within_section,
        ((rows, width), F32),
        own_bc, other_bc, x, segment, skip_wide, message,
        flops=3 * flops(rows, rows, width),
    )
    gate = run(
        functools.partial(last_z, masks),
        ((rows, width), F32),
        *ends, weights, sums, message,
        flops=flops(rows, depth, width),
    )
    keep, give = run(
        entering_state, [(state_shape, BF16), (state_shape, BF16)], kept, whole, received, *got, within, gate
    )
    take = partner(give, "ctx", 1)
    gated, square = run(
        gated_output,
        [((rows, width), F32), ((ROWS, rows), F32)],
        own_bc, other_bc, keep, take, within, grown, gate,
        flops=flops(rows, n, width),
    )
    other_square = partner(square, "tp", 1)
    return run(
        normed_output, ((rows, width), BF16), gated, square, other_square, gain.reshape(1, -1)
    )


def solution(mesh):
    in_specs = (
        P("ctx", "tp"),
        P(None, "tp"),
        P(None, "tp"),
        P(None, "tp"),
        P(None, "tp"),
        P(None, "tp"),
        P("tp"),
        P("tp"),
        P("ctx", "tp"),
        P("tp"),
        P("tp"),
        P("tp"),
    )
    out_specs = P("ctx", "tp")
    return jax.shard_map(local, mesh=mesh, in_specs=in_specs, out_specs=out_specs, check_vma=False)
```

```python
import functools

import jax
import jax.numpy as jnp
from jax import lax
from jax.experimental import pallas as pl
from jax.experimental.pallas import tpu as pltpu
from jax.sharding import PartitionSpec as P


KERNEL = 4
UPPER = 8
RIM = 8
ROWS = 8
PAD = 4
F32, BF16 = jnp.float32, jnp.bfloat16
EXACT = lax.Precision.HIGHEST
VMEM = pl.BlockSpec(memory_space=pltpu.VMEM)
HBM = pl.BlockSpec(memory_space=pltpu.HBM)


def run(body, outs, *operands, scratch=(), flops=1000000, hbm=0, limit=4 << 20):
    single = not isinstance(outs, list)
    shapes = [jax.ShapeDtypeStruct(*o) for o in ([outs] if single else outs)]
    operands = [
        pltpu.with_memory_space_constraint(o, pltpu.HBM) if i < hbm else o
        for i, o in enumerate(operands)
    ]
    call = pl.pallas_call(
        body,
        out_shape=shapes,
        in_specs=[HBM] * hbm + [VMEM] * (len(operands) - hbm),
        out_specs=[VMEM] * len(shapes),
        scratch_shapes=list(scratch),
        compiler_params=pltpu.CompilerParams(vmem_limit_bytes=limit),
        cost_estimate=pl.CostEstimate(flops=flops, bytes_accessed=flops // 400, transcendentals=0),
    )
    results = call(*operands)
    return results[0] if single else results


def partner(value, axis, mask):
    return lax.ppermute(value, axis, [(i, i ^ mask) for i in range(lax.axis_size(axis))])


def across_chips(value, mask):
    return partner(value, "ctx", 2 * mask)


def onward(value, axis):
    size = lax.axis_size(axis)
    return lax.ppermute(value, axis, [(i, (i + 1) % size) for i in range(size)])


def dot(a, b, **kwargs):
    return jnp.dot(a, b, preferred_element_type=F32, **kwargs)


def silu(v):
    return v / (1.0 + jnp.exp(-v))


def holds_b():
    return lax.axis_index("tp") % 2 == 0


def first_core():
    return lax.axis_index("ctx") % 2 == 0


def fetched_halves(source, top, bottom, rim, arrivals):
    rows = source.shape[0]
    copies = [
        pltpu.make_async_copy(source.at[pl.ds(start, out.shape[0])], out, arrivals.at[i])
        for i, (start, out) in enumerate(((top.shape[0], bottom), (0, top), (rows - RIM, rim)))
    ]
    for copy in copies:
        copy.start()
    for copy in copies:
        copy.wait()


def weight_copies(sources, weights, arrivals, masks):
    depth = weights.shape[1]
    copies = []
    for slot, mask in enumerate(masks):
        start = pl.multiple_of(jnp.bitwise_xor(lax.axis_index("tp"), mask) * depth, depth)
        column = 0
        for i, w in enumerate(sources):
            there = weights.at[slot, :, pl.ds(column, w.shape[1])]
            copies.append(
                pltpu.make_async_copy(w.at[pl.ds(start, depth)], there, arrivals.at[slot, i])
            )
            column += w.shape[1]
    for copy in copies:
        copy.start()
    return copies


def last_weights(masks, w_bc, w_x, w_z, weights, arrivals):
    for copy in weight_copies((w_bc, w_x, w_z), weights, arrivals, masks):
        copy.wait()


def own_product(masks, w_bc, w_x, w_z, top, bottom, sums, weights, arrivals):
    copies = weight_copies((w_bc, w_x, w_z), weights, arrivals, masks)
    for copy in copies[:3]:
        copy.wait()
    sums[...] = dot(jnp.concatenate([top[...], bottom[...]], axis=0), weights[0])
    for copy in copies[3:]:
        copy.wait()


def block_of(pieces, i):
    return jnp.concatenate([pieces[2 * i][...], pieces[2 * i + 1][...]], axis=0)


def middle_product(masks, *refs):
    pieces, (weights, before, out) = refs[: 2 * len(masks)], refs[2 * len(masks) :]
    total = before[...]
    for i, mask in enumerate(masks):
        total += dot(block_of(pieces, i), weights[mask])
    out[...] = total


def rim_product(*refs):
    pieces, (early, last, out) = refs[:-3], refs[-3:]
    columns = pl.ds(0, out.shape[1])
    total = None
    for mask, piece in enumerate(pieces):
        count = early.shape[0]
        part = early[mask, :, columns] if mask < count else last[mask - count, :, columns]
        term = dot(piece[...], part)
        total = term if total is None else total + term
    inside = lax.axis_index("ctx") > 0
    out[...] = jnp.where(inside, total, 0.0).astype(BF16).astype(F32)


def finished(masks, pieces, weights, before, start, width):
    columns = pl.ds(start, width)
    total = before[:, columns]
    for i in range(len(masks)):
        total += dot(block_of(pieces, i), weights[i, :, columns])
    return total.astype(BF16).astype(F32)


def convolved(pre, rim, taps, bias, extended):
    rows = pre.shape[0]
    extended[pl.ds(0, RIM), :] = rim
    extended[pl.ds(RIM, rows), :] = pre
    total = bias[...]
    for k in range(KERNEL):
        total = total + taps[pl.ds(k, 1), :] * extended[pl.ds(RIM - KERNEL + 1 + k, rows), :]
    return silu(total).astype(BF16)


def last_bc(masks, *refs):
    pieces, refs = refs[: 2 * len(masks)], refs[2 * len(masks) :]
    weights, before, rim, taps, bias, out, extended = refs
    width = out.shape[1]
    pre = finished(masks, pieces, weights, before, 0, width)
    out[...] = convolved(pre, rim[:, pl.ds(0, width)], taps, bias, extended)


def last_x(masks, *refs):
    pieces, refs = refs[: 2 * len(masks)], refs[2 * len(masks) :]
    weights, before, rim, taps, bias, end_weight, x_out, weighted_out, extended = refs
    width = x_out.shape[1]
    start = rim.shape[1] - width
    pre = finished(masks, pieces, weights, before, start, width)
    x = convolved(pre, rim[:, pl.ds(start, width)], taps, bias, extended)
    x_out[...] = x
    weighted_out[...] = (x.astype(F32) * end_weight[...]).astype(BF16)


def last_z(masks, *refs):
    pieces, (weights, before, _, out) = refs[: 2 * len(masks)], refs[2 * len(masks) :]
    width = out.shape[1]
    out[...] = silu(finished(masks, pieces, weights, before, before.shape[1] - width, width))


def decays(*refs):
    sources, refs = refs[:3], refs[3:]
    segment, grown, end_weight, whole, skip_wide, *held, arrivals = refs
    copies = [
        pltpu.make_async_copy(source, there, arrivals.at[i])
        for i, (source, there) in enumerate(zip(sources, held))
    ]
    for copy in copies:
        copy.start()
    for copy in copies:
        copy.wait()
    decay_t, step, skip = held
    heads, rows = decay_t.shape
    width = grown.shape[1]
    dim = width // heads
    spread = (
        lax.broadcasted_iota(jnp.int32, (heads, width), 1) // dim
        == lax.broadcasted_iota(jnp.int32, (heads, width), 0)
    ).astype(F32)
    i = lax.broadcasted_iota(jnp.int32, (rows, rows), 0)
    j = lax.broadcasted_iota(jnp.int32, (rows, rows), 1)
    causal = i >= j
    cum = lax.dot_general(
        causal.astype(F32),
        decay_t[...],
        (((1,), (1,)), ((), ())),
        precision=EXACT,
        preferred_element_type=F32,
    )
    cum_t = dot(decay_t[...], (i <= j).astype(F32), precision=EXACT)
    cum_wide = dot(cum, spread, precision=EXACT)
    total = cum_wide[rows - 1 :]
    grown[...] = jnp.exp(cum_wide)
    end_weight[...] = jnp.exp(total - cum_wide) * dot(step[...], spread, precision=EXACT)
    whole[...] = jnp.broadcast_to(jnp.exp(total), whole.shape)
    skip_wide[...] = dot(skip[...], spread, precision=EXACT)
    for h in range(heads):
        difference = cum[:, h : h + 1] - cum_t[h : h + 1, :]
        factor = jnp.where(causal, jnp.exp(jnp.where(causal, difference, 0.0)), 0.0)
        segment[h] = (factor * step[:, h : h + 1]).astype(BF16)


def halves(wide):
    half = wide.shape[1] // 2
    return wide[:, :half], wide[:, half:]


def mine_other(wide):
    low, high = halves(wide)
    first = first_core()
    return jnp.where(first, low, high), jnp.where(first, high, low)


def write_message(out, state, decay):
    n = state.shape[0]
    out[pl.ds(0, n), :] = state.astype(BF16)
    decay = jnp.broadcast_to(decay, (PAD, decay.shape[1]))
    high = decay.astype(BF16).astype(F32)
    out[pl.ds(n, 2 * PAD), :] = jnp.concatenate([high, decay - high], axis=0).astype(BF16)


def read_message(ref):
    n = ref.shape[0] - 2 * PAD
    tail = ref[pl.ds(n, 2 * PAD), :].astype(F32)
    return ref[pl.ds(0, n), :].astype(F32), tail[:1] + tail[PAD : PAD + 1]


def section_state(own_bc, other_bc, weighted, whole, message, kept):
    b = jnp.where(holds_b(), own_bc[...], other_bc[...])
    state = lax.dot_general(
        b, weighted[...], (((0,), (0,)), ((), ())), preferred_element_type=F32
    )
    mine, other = mine_other(state)
    _, other_decay = mine_other(whole[...])
    kept[...] = mine
    write_message(message, other, other_decay[:1])


def pair_states(kept, whole, received):
    sibling, sibling_decay = read_message(received)
    mine_decay, _ = mine_other(whole[...])
    mine_decay = mine_decay[:1]
    first = first_core()
    mine = kept[...]
    return (
        (jnp.where(first, mine, sibling), jnp.where(first, mine_decay, sibling_decay)),
        (jnp.where(first, sibling, mine), jnp.where(first, sibling_decay, mine_decay)),
    )


def chip_state(kept, whole, received, message):
    (first, first_decay), (second, second_decay) = pair_states(kept, whole, received)
    write_message(message, second + second_decay * first, first_decay * second_decay)


def entering_state(kept, whole, received, *refs):
    got, (_, _, keep, give) = refs[:-4], refs[-4:]
    (first, first_decay), _ = pair_states(kept, whole, received)
    chip = lax.axis_index("ctx") // 2
    messages = [read_message(ref) for ref in got]
    places = [jnp.bitwise_xor(chip, mask) for mask in range(1, len(got) + 1)]
    before = jnp.zeros_like(first)
    for place, (state, _) in zip(places, messages):
        weight = jnp.ones_like(first_decay)
        for other, (_, decay) in zip(places, messages):
            weight *= jnp.where((other > place) & (other < chip), decay, 1.0)
        before += jnp.where(place < chip, weight, 0.0) * state
    after = first + first_decay * before
    lead = first_core()
    keep[...] = jnp.where(lead, before, after).astype(BF16)
    give[...] = jnp.where(lead, after, before).astype(BF16)


def within_section(own_bc, other_bc, x, segment, skip_wide, _, out):
    own, other = own_bc[...], other_bc[...]
    b = jnp.where(holds_b(), own, other)
    c = jnp.where(holds_b(), other, own)
    scores = lax.dot_general(c, b, (((1,), (1,)), ((), ())), preferred_element_type=F32)
    heads = segment.shape[0]
    dim = x.shape[1] // heads
    low = lax.broadcasted_iota(jnp.int32, (1, 2 * dim), 1) < dim
    for pair in range(heads // 2):
        columns = pl.ds(pair * 2 * dim, 2 * dim)
        mixing = jnp.concatenate(
            [(segment[2 * pair + s].astype(F32) * scores).astype(BF16) for s in range(2)], axis=1
        )
        both = x[:, columns]
        wide = both.astype(F32)
        stacked = jnp.concatenate(
            [jnp.where(low, wide, 0.0).astype(BF16), jnp.where(low, 0.0, wide).astype(BF16)], axis=0
        )
        out[:, columns] = dot(mixing, stacked) + skip_wide[:, columns] * wide


def gated_output(own_bc, other_bc, keep, take, within, grown, gate, gated_out, square_out):
    lead = first_core()
    low = jnp.where(lead, keep[...], take[...])
    high = jnp.where(lead, take[...], keep[...])
    c = jnp.where(holds_b(), other_bc[...], own_bc[...])
    half = low.shape[1]
    squares = None
    for s, entering in enumerate((low, high)):
        columns = pl.ds(s * half, half)
        inter = dot(c, entering) * grown[:, columns]
        gated = (within[:, columns] + inter) * gate[:, columns]
        gated_out[:, columns] = gated
        for start in range(0, half, 128):
            part = gated[:, start : start + 128]
            squares = part * part if squares is None else squares + part * part
    ones = jnp.ones((ROWS, squares.shape[1]), F32)
    square_out[...] = lax.dot_general(
        ones, squares, (((1,), (1,)), ((), ())), precision=EXACT, preferred_element_type=F32
    )


def normed_output(gated, square, other_square, gain, out):
    width = gated.shape[1]
    mean = (square[...] + other_square[...]) / (2 * width)
    factor = lax.rsqrt(mean + 1e-05)
    share = jnp.full((ROWS, 128), 1.0 / ROWS, F32)
    column = lax.dot_general(
        factor, share, (((0,), (0,)), ((), ())), precision=EXACT, preferred_element_type=F32
    )
    for start in range(0, width, 128):
        columns = pl.ds(start, 128)
        out[:, columns] = (gated[:, columns] * column * gain[:, columns]).astype(BF16)


def gather_pieces(top, bottom, axis):
    size = lax.axis_size(axis)
    near_bottom = partner(bottom, axis, 1)
    far_top = partner(top, axis, 2)
    near_top = partner(top, axis, 1)
    far_bottom = partner(bottom, axis, 2)
    across_bottom = partner(near_bottom, axis, 2)
    across_top = partner(far_top, axis, 1)
    early = {1: [near_top, near_bottom], 2: [far_top, far_bottom]}
    last = {3: [across_top, across_bottom]}
    mask = 4
    while mask < size:
        early = {**early, **last}
        last = {m | mask: [partner(h, axis, mask) for h in p] for m, p in early.items()}
        last[mask] = [partner(h, axis, mask) for h in (top, bottom)]
        mask *= 2
    return early, last


def gather_rim(rim, axis):
    pieces = [onward(rim, "ctx")]
    for mask in range(1, lax.axis_size(axis)):
        pieces.append(partner(pieces[0], axis, mask))
    return pieces


def local(
    tokens, w_z, w_x, w_bc, conv_x, conv_bc, bias_x, bias_bc, decay_logarithm, head_step, skip, gain
):
    rows, depth = tokens.shape
    width, bc_width = w_x.shape[1], w_bc.shape[1]
    heads = head_step.shape[0]
    n = bc_width
    chips = lax.axis_size("ctx") // 2

    upper = rows * UPPER // 16
    top, bottom, rim = run(
        fetched_halves,
        [((upper, depth), BF16), ((rows - upper, depth), BF16), ((RIM, depth), BF16)],
        tokens,
        scratch=[pltpu.SemaphoreType.DMA((3,))],
        hbm=1,
    )

    def flops(*sizes):
        total = 2
        for s in sizes:
            total *= s
        return total

    early, last = gather_pieces(top, bottom, "tp")
    rims = gather_rim(rim, "tp")
    everything = bc_width + 2 * width
    masks = (0, *sorted(early))
    sums, weights = run(
        functools.partial(own_product, masks),
        [((rows, everything), F32), ((len(masks), depth, everything), BF16)],
        w_bc, w_x, w_z, top, bottom,
        scratch=[pltpu.SemaphoreType.DMA((len(masks), 3))],
        flops=flops(rows, depth, everything),
        hbm=3,
    )
    masks = tuple(sorted(last))
    weights_end = run(
        functools.partial(last_weights, masks),
        ((len(masks), depth, everything), BF16),
        w_bc, w_x, w_z,
        scratch=[pltpu.SemaphoreType.DMA((len(masks), 3))],
        hbm=3,
    )
    segment, grown, end_weight, whole, skip_wide = run(
        decays,
        [
            ((heads, rows, rows), BF16),
            ((rows, width), F32),
            ((rows, width), F32),
            ((ROWS, width), F32),
            ((1, width), F32),
        ],
        decay_logarithm.T, head_step.reshape(1, -1), skip.reshape(1, -1),
        scratch=[
            pltpu.VMEM((heads, rows), F32),
            pltpu.VMEM((1, heads), F32),
            pltpu.VMEM((1, heads), F32),
            pltpu.SemaphoreType.DMA((3,)),
        ],
        hbm=3,
        flops=flops(rows, rows, width),
    )
    masks = tuple(sorted(early))
    sums = run(
        functools.partial(middle_product, masks),
        ((rows, everything), F32),
        *[h for m in masks for h in early[m]], weights, sums,
        flops=len(masks) * flops(rows, depth, everything),
    )
    rim_sums = run(
        rim_product,
        ((RIM, bc_width + width), F32),
        *rims, weights, weights_end,
        flops=flops(rows, depth, width),
    )

    masks = tuple(sorted(last))
    ends = [h for m in masks for h in last[m]]
    own_bc = run(
        functools.partial(last_bc, masks),
        ((rows, bc_width), BF16),
        *ends, weights_end, sums, rim_sums, conv_bc, bias_bc.reshape(1, -1),
        scratch=[pltpu.VMEM((rows + RIM, bc_width), F32)],
        flops=flops(rows, depth, bc_width),
    )
    other_bc = partner(own_bc, "tp", 1)
    x, weighted = run(
        functools.partial(last_x, masks),
        [((rows, width), BF16), ((rows, width), BF16)],
        *ends, weights_end, sums, rim_sums, conv_x, bias_x.reshape(1, -1), end_weight,
        scratch=[pltpu.VMEM((rows + RIM, width), F32)],
        flops=flops(rows, depth, width),
    )
    message_shape = ((n + 2 * PAD, width // 2), BF16)
    state_shape = (n, width // 2)
    message, kept = run(
        section_state,
        [message_shape, (state_shape, F32)],
        own_bc, other_bc, weighted, whole,
        flops=flops(rows, n, width),
    )
    received = partner(message, "ctx", 1)
    message = run(chip_state, message_shape, kept, whole, received)
    got = []
    for mask in range(1, chips):
        got.append(across_chips(message, mask))
    within = run(
        within_section,
        ((rows, width), F32),
        own_bc, other_bc, x, segment, skip_wide, message,
        flops=3 * flops(rows, rows, width),
    )
    gate = run(
        functools.partial(last_z, masks),
        ((rows, width), F32),
        *ends, weights_end, sums, message,
        flops=flops(rows, depth, width),
    )
    keep, give = run(
        entering_state, [(state_shape, BF16), (state_shape, BF16)], kept, whole, received, *got, within, gate
    )
    take = partner(give, "ctx", 1)
    gated, square = run(
        gated_output,
        [((rows, width), F32), ((ROWS, rows), F32)],
        own_bc, other_bc, keep, take, within, grown, gate,
        flops=flops(rows, n, width),
    )
    other_square = partner(square, "tp", 1)
    return run(
        normed_output, ((rows, width), BF16), gated, square, other_square, gain.reshape(1, -1)
    )


def solution(mesh):
    in_specs = (
        P("ctx", "tp"),
        P(None, "tp"),
        P(None, "tp"),
        P(None, "tp"),
        P(None, "tp"),
        P(None, "tp"),
        P("tp"),
        P("tp"),
        P("ctx", "tp"),
        P("tp"),
        P("tp"),
        P("tp"),
    )
    out_specs = P("ctx", "tp")
    return jax.shard_map(local, mesh=mesh, in_specs=in_specs, out_specs=out_specs, check_vma=False)
```

```python
import functools

import jax
import jax.numpy as jnp
from jax import lax
from jax.experimental import pallas as pl
from jax.experimental.pallas import tpu as pltpu
from jax.sharding import PartitionSpec as P


KERNEL = 4
UPPER = 9
RIM = 8
ROWS = 8
CHUNKS = 4
PAD = 4
F32, BF16 = jnp.float32, jnp.bfloat16
EXACT = lax.Precision.HIGHEST
VMEM = pl.BlockSpec(memory_space=pltpu.VMEM)
HBM = pl.BlockSpec(memory_space=pltpu.HBM)


def run(body, outs, *operands, scratch=(), flops=1000000, hbm=0, out=VMEM, limit=4 << 20):
    single = not isinstance(outs, list)
    shapes = [jax.ShapeDtypeStruct(*o) for o in ([outs] if single else outs)]
    operands = [
        pltpu.with_memory_space_constraint(o, pltpu.HBM) if i < hbm else o
        for i, o in enumerate(operands)
    ]
    call = pl.pallas_call(
        body,
        out_shape=shapes,
        in_specs=[HBM] * hbm + [VMEM] * (len(operands) - hbm),
        out_specs=[out] * len(shapes),
        scratch_shapes=list(scratch),
        compiler_params=pltpu.CompilerParams(vmem_limit_bytes=limit),
        cost_estimate=pl.CostEstimate(flops=flops, bytes_accessed=flops // 400, transcendentals=0),
    )
    results = call(*operands)
    return results[0] if single else results


def partner(value, axis, mask):
    return lax.ppermute(value, axis, [(i, i ^ mask) for i in range(lax.axis_size(axis))])


def across_chips(value, mask):
    return partner(value, "ctx", 2 * mask)


def onward(value, axis):
    size = lax.axis_size(axis)
    return lax.ppermute(value, axis, [(i, (i + 1) % size) for i in range(size)])


def dot(a, b, **kwargs):
    return jnp.dot(a, b, preferred_element_type=F32, **kwargs)


def two_parts(value):
    high = value.astype(BF16)
    return high, (value - high.astype(F32)).astype(BF16)


def silu(v):
    return v / (1.0 + jnp.exp(-v))


def holds_b():
    return lax.axis_index("tp") % 2 == 0


def first_core():
    return lax.axis_index("ctx") % 2 == 0


def whole_copies(sources, targets, arrivals, first):
    copies = [
        pltpu.make_async_copy(source, target, arrivals.at[first + i])
        for i, (source, target) in enumerate(zip(sources, targets))
    ]
    for copy in copies:
        copy.start()
    return copies


def fetched_halves(source, *refs):
    count = (len(refs) - 4) // 2
    small, (top, bottom, rim, *held, arrivals) = refs[:count], refs[count:]
    rows = source.shape[0]
    copies = [
        pltpu.make_async_copy(source.at[pl.ds(start, out.shape[0])], out, arrivals.at[i])
        for i, (start, out) in enumerate(((top.shape[0], bottom), (0, top), (rows - RIM, rim)))
    ]
    for copy in copies:
        copy.start()
    for copy in copies + whole_copies(small, held, arrivals, 3):
        copy.wait()


def weight_copies(sources, weights, arrivals, masks):
    depth = weights.shape[1]
    copies = []
    for slot, mask in enumerate(masks):
        start = pl.multiple_of(jnp.bitwise_xor(lax.axis_index("tp"), mask) * depth, depth)
        column = 0
        for i, w in enumerate(sources):
            there = weights.at[slot, :, pl.ds(column, w.shape[1])]
            copies.append(
                pltpu.make_async_copy(w.at[pl.ds(start, depth)], there, arrivals.at[slot, i])
            )
            column += w.shape[1]
    for copy in copies:
        copy.start()
    return copies


def last_weights(masks, w_bc, w_x, w_z, *refs):
    count = (len(refs) - 3) // 2
    small, (weights, *held, arrivals, small_arrivals) = refs[:count], refs[count:]
    copies = weight_copies((w_bc, w_x, w_z), weights, arrivals, masks)
    for copy in copies + whole_copies(small, held, small_arrivals, 0):
        copy.wait()


def own_product(masks, w_bc, w_x, w_z, top, bottom, sums, weights, arrivals):
    copies = weight_copies((w_bc, w_x, w_z), weights, arrivals, masks)
    for copy in copies[:3]:
        copy.wait()
    sums[...] = dot(jnp.concatenate([top[...], bottom[...]], axis=0), weights[0])
    for copy in copies[3:]:
        copy.wait()


def block_of(pieces, i):
    return jnp.concatenate([pieces[2 * i][...], pieces[2 * i + 1][...]], axis=0)


def middle_product(masks, *refs):
    pieces, (weights, before, out) = refs[: 2 * len(masks)], refs[2 * len(masks) :]
    total = before[...]
    for i, mask in enumerate(masks):
        total += dot(block_of(pieces, i), weights[mask])
    out[...] = total


def rim_product(*refs):
    pieces, (early, last, out) = refs[:-3], refs[-3:]
    columns = pl.ds(0, out.shape[1])
    total = None
    for mask, piece in enumerate(pieces):
        count = early.shape[0]
        part = early[mask, :, columns] if mask < count else last[mask - count, :, columns]
        term = dot(piece[...], part)
        total = term if total is None else total + term
    inside = lax.axis_index("ctx") > 0
    out[...] = jnp.where(inside, total, 0.0).astype(BF16).astype(F32)


def finished(masks, pieces, weights, before, start, width):
    columns = pl.ds(start, width)
    total = before[:, columns]
    for i in range(len(masks)):
        total += dot(block_of(pieces, i), weights[i, :, columns])
    return total.astype(BF16).astype(F32)


def convolved(pre, rim, taps, bias, extended):
    rows = pre.shape[0]
    extended[pl.ds(0, RIM), :] = rim
    extended[pl.ds(RIM, rows), :] = pre
    total = bias[...]
    for k in range(KERNEL):
        total = total + taps[pl.ds(k, 1), :] * extended[pl.ds(RIM - KERNEL + 1 + k, rows), :]
    return silu(total).astype(BF16)


def last_bc(masks, *refs):
    pieces, refs = refs[: 2 * len(masks)], refs[2 * len(masks) :]
    weights, before, rim, taps, bias, out, extended = refs
    width = out.shape[1]
    pre = finished(masks, pieces, weights, before, 0, width)
    out[...] = convolved(pre, rim[:, pl.ds(0, width)], taps, bias, extended)


def last_x(masks, *refs):
    pieces, refs = refs[: 2 * len(masks)], refs[2 * len(masks) :]
    weights, before, rim, taps, bias, end_weight, x_out, weighted_out, extended = refs
    width = x_out.shape[1]
    start = rim.shape[1] - width
    pre = finished(masks, pieces, weights, before, start, width)
    x = convolved(pre, rim[:, pl.ds(start, width)], taps, bias, extended)
    x_out[...] = x
    weighted_out[...] = (x.astype(F32) * end_weight[...]).astype(BF16)


def last_z(masks, *refs):
    pieces, (weights, before, _, out) = refs[: 2 * len(masks)], refs[2 * len(masks) :]
    width = out.shape[1]
    out[...] = silu(finished(masks, pieces, weights, before, before.shape[1] - width, width))


def decays(decay_t, step, skip, segment, grown, end_weight, whole, skip_wide):
    heads, rows = decay_t.shape
    width = grown.shape[1]
    dim = width // heads
    spread = (
        lax.broadcasted_iota(jnp.int32, (heads, width), 1) // dim
        == lax.broadcasted_iota(jnp.int32, (heads, width), 0)
    ).astype(F32)
    i = lax.broadcasted_iota(jnp.int32, (rows, rows), 0)
    j = lax.broadcasted_iota(jnp.int32, (rows, rows), 1)
    causal = i >= j
    cum = lax.dot_general(
        causal.astype(F32),
        decay_t[...],
        (((1,), (1,)), ((), ())),
        precision=EXACT,
        preferred_element_type=F32,
    )
    cum_t = dot(decay_t[...], (i <= j).astype(F32), precision=EXACT)
    cum_wide = dot(cum, spread, precision=EXACT)
    total = cum_wide[rows - 1 :]
    grown[...] = jnp.exp(cum_wide)
    end_weight[...] = jnp.exp(total - cum_wide) * dot(step[...], spread, precision=EXACT)
    whole[...] = jnp.broadcast_to(jnp.exp(total), whole.shape)
    skip_wide[...] = dot(skip[...], spread, precision=EXACT)
    for h in range(heads):
        difference = cum[:, h : h + 1] - cum_t[h : h + 1, :]
        factor = jnp.where(causal, jnp.exp(jnp.where(causal, difference, 0.0)), 0.0)
        segment[h] = (factor * step[:, h : h + 1]).astype(BF16)


def halves(wide):
    half = wide.shape[1] // 2
    return wide[:, :half], wide[:, half:]


def mine_other(wide):
    low, high = halves(wide)
    first = first_core()
    return jnp.where(first, low, high), jnp.where(first, high, low)


def write_message(out, state, decay):
    n = state.shape[0]
    out[pl.ds(0, n), :] = state.astype(BF16)
    decay = jnp.broadcast_to(decay, (PAD, decay.shape[1]))
    high = decay.astype(BF16).astype(F32)
    out[pl.ds(n, 2 * PAD), :] = jnp.concatenate([high, decay - high], axis=0).astype(BF16)


def read_message(ref):
    n = ref.shape[0] - 2 * PAD
    tail = ref[pl.ds(n, 2 * PAD), :].astype(F32)
    return ref[pl.ds(0, n), :].astype(F32), tail[:1] + tail[PAD : PAD + 1]


def section_state(own_bc, other_bc, weighted, whole, message, kept):
    b = jnp.where(holds_b(), own_bc[...], other_bc[...])
    state = lax.dot_general(
        b, weighted[...], (((0,), (0,)), ((), ())), preferred_element_type=F32
    )
    mine, other = mine_other(state)
    _, other_decay = mine_other(whole[...])
    kept[...] = mine
    write_message(message, other, other_decay[:1])


def pair_states(kept, whole, received):
    sibling, sibling_decay = read_message(received)
    mine_decay, _ = mine_other(whole[...])
    mine_decay = mine_decay[:1]
    first = first_core()
    mine = kept[...]
    return (
        (jnp.where(first, mine, sibling), jnp.where(first, mine_decay, sibling_decay)),
        (jnp.where(first, sibling, mine), jnp.where(first, sibling_decay, mine_decay)),
    )


def chip_state(kept, whole, received, message):
    (first, first_decay), (second, second_decay) = pair_states(kept, whole, received)
    write_message(message, second + second_decay * first, first_decay * second_decay)


def entering_state(kept, whole, received, *refs):
    got, (_, _, keep, give) = refs[:-4], refs[-4:]
    (first, first_decay), _ = pair_states(kept, whole, received)
    chip = lax.axis_index("ctx") // 2
    messages = [read_message(ref) for ref in got]
    places = [jnp.bitwise_xor(chip, mask) for mask in range(1, len(got) + 1)]
    before = jnp.zeros_like(first)
    for place, (state, _) in zip(places, messages):
        weight = jnp.ones_like(first_decay)
        for other, (_, decay) in zip(places, messages):
            weight *= jnp.where((other > place) & (other < chip), decay, 1.0)
        before += jnp.where(place < chip, weight, 0.0) * state
    after = first + first_decay * before
    lead = first_core()
    keep[...] = jnp.where(lead, before, after).astype(BF16)
    give[...] = jnp.where(lead, after, before).astype(BF16)


def within_section(own_bc, other_bc, x, segment, skip_wide, _, out):
    own, other = own_bc[...], other_bc[...]
    b = jnp.where(holds_b(), own, other)
    c = jnp.where(holds_b(), other, own)
    scores = lax.dot_general(c, b, (((1,), (1,)), ((), ())), preferred_element_type=F32)
    heads = segment.shape[0]
    dim = x.shape[1] // heads
    low = lax.broadcasted_iota(jnp.int32, (1, 2 * dim), 1) < dim
    for pair in range(heads // 2):
        columns = pl.ds(pair * 2 * dim, 2 * dim)
        mixing = jnp.concatenate(
            [(segment[2 * pair + s].astype(F32) * scores).astype(BF16) for s in range(2)], axis=1
        )
        both = x[:, columns]
        wide = both.astype(F32)
        stacked = jnp.concatenate(
            [jnp.where(low, wide, 0.0).astype(BF16), jnp.where(low, 0.0, wide).astype(BF16)], axis=0
        )
        out[:, columns] = dot(mixing, stacked) + skip_wide[:, columns] * wide


def gated_half(c, state, start, within, grown, gate):
    half = state.shape[1]
    columns = pl.ds(start, half)
    gated = (within[:, columns] + dot(c, state) * grown[:, columns]) * gate[:, columns]
    squares = None
    for lane in range(0, half, 128):
        part = gated[:, lane : lane + 128]
        squares = part * part if squares is None else squares + part * part
    return gated, squares


def half_starts(half):
    core = lax.axis_index("ctx") % 2
    return [pl.multiple_of(place * half, 128) for place in (core, 1 - core)]


def gated_mine(own_bc, other_bc, keep, within, grown, gate, gated_out, squares_out):
    c = jnp.where(holds_b(), other_bc[...], own_bc[...])
    mine, _ = half_starts(keep.shape[1])
    gated_out[...], squares_out[...] = gated_half(c, keep[...], mine, within, grown, gate)


def gated_other(own_bc, other_bc, take, within, grown, gate, squares, gated_out, square_out):
    c = jnp.where(holds_b(), other_bc[...], own_bc[...])
    _, other = half_starts(take.shape[1])
    gated_out[...], more = gated_half(c, take[...], other, within, grown, gate)
    ones = jnp.ones((ROWS, more.shape[1]), BF16)
    square_out[...] = sum(
        lax.dot_general(ones, part, (((1,), (1,)), ((), ())), preferred_element_type=F32)
        for part in two_parts(squares[...] + more)
    )


def normed_output(mine, other, square, other_square, gain, out, held, sent):
    rows, half = mine.shape
    mean = (square[...] + other_square[...]) / (4 * half)
    share = jnp.full((ROWS, 128), 1.0 / ROWS, BF16)
    factor = sum(
        lax.dot_general(part, share, (((0,), (0,)), ((), ())), preferred_element_type=F32)
        for part in two_parts(lax.rsqrt(mean + 1e-05))
    )
    copies = []
    count = rows // CHUNKS
    for chunk in range(CHUNKS):
        some = pl.ds(chunk * count, count)
        column = factor[chunk * count : (chunk + 1) * count]
        for gated, start in zip((mine, other), half_starts(half)):
            for lane in range(0, half, 128):
                columns = pl.ds(pl.multiple_of(start + lane, 128), 128)
                wide = gated[some, pl.ds(lane, 128)] * column * gain[:, columns]
                held[some, columns] = wide.astype(BF16)
        copies.append(pltpu.make_async_copy(held.at[some], out.at[some], sent.at[chunk]))
        copies[-1].start()
    for copy in copies:
        copy.wait()


def gather_pieces(top, bottom, axis):
    size = lax.axis_size(axis)
    near_bottom = partner(bottom, axis, 1)
    far_top = partner(top, axis, 2)
    near_top = partner(top, axis, 1)
    far_bottom = partner(bottom, axis, 2)
    across_bottom = partner(near_bottom, axis, 2)
    across_top = partner(far_top, axis, 1)
    early = {1: [near_top, near_bottom], 2: [far_top, far_bottom]}
    last = {3: [across_top, across_bottom]}
    mask = 4
    while mask < size:
        early = {**early, **last}
        last = {m | mask: [partner(h, axis, mask) for h in p] for m, p in early.items()}
        last[mask] = [partner(h, axis, mask) for h in (top, bottom)]
        mask *= 2
    return early, last


def gather_rim(rim, axis):
    pieces = [onward(rim, "ctx")]
    for mask in range(1, lax.axis_size(axis)):
        pieces.append(partner(pieces[0], axis, mask))
    return pieces


def local(
    tokens, w_z, w_x, w_bc, conv_x, conv_bc, bias_x, bias_bc, decay_logarithm, head_step, skip, gain
):
    rows, depth = tokens.shape
    width, bc_width = w_x.shape[1], w_bc.shape[1]
    heads = head_step.shape[0]
    n = bc_width
    chips = lax.axis_size("ctx") // 2

    upper = rows * UPPER // 16
    small = (decay_logarithm.T, head_step.reshape(1, -1), skip.reshape(1, -1))
    top, bottom, rim, *small = run(
        fetched_halves,
        [
            ((upper, depth), BF16),
            ((rows - upper, depth), BF16),
            ((RIM, depth), BF16),
            *[(a.shape, F32) for a in small],
        ],
        tokens, *small,
        scratch=[pltpu.SemaphoreType.DMA((3 + len(small),))],
        hbm=1 + len(small),
    )

    def flops(*sizes):
        total = 2
        for s in sizes:
            total *= s
        return total

    early, last = gather_pieces(top, bottom, "tp")
    rims = gather_rim(rim, "tp")
    everything = bc_width + 2 * width
    masks = (0, *sorted(early))
    sums, weights = run(
        functools.partial(own_product, masks),
        [((rows, everything), F32), ((len(masks), depth, everything), BF16)],
        w_bc, w_x, w_z, top, bottom,
        scratch=[pltpu.SemaphoreType.DMA((len(masks), 3))],
        flops=flops(rows, depth, everything),
        hbm=3,
    )
    masks = tuple(sorted(last))
    vectors = (conv_bc, bias_bc.reshape(1, -1), conv_x, bias_x.reshape(1, -1), gain.reshape(1, -1))
    weights_end, conv_bc, bias_bc, conv_x, bias_x, gain = run(
        functools.partial(last_weights, masks),
        [((len(masks), depth, everything), BF16), *[(v.shape, F32) for v in vectors]],
        w_bc, w_x, w_z, *vectors,
        scratch=[
            pltpu.SemaphoreType.DMA((len(masks), 3)),
            pltpu.SemaphoreType.DMA((len(vectors),)),
        ],
        hbm=3 + len(vectors),
    )
    segment, grown, end_weight, whole, skip_wide = run(
        decays,
        [
            ((heads, rows, rows), BF16),
            ((rows, width), F32),
            ((rows, width), F32),
            ((ROWS, width), F32),
            ((1, width), F32),
        ],
        *small,
        flops=flops(rows, rows, width),
    )
    masks = tuple(sorted(early))
    sums = run(
        functools.partial(middle_product, masks),
        ((rows, everything), F32),
        *[h for m in masks for h in early[m]], weights, sums,
        flops=len(masks) * flops(rows, depth, everything),
    )
    rim_sums = run(
        rim_product,
        ((RIM, bc_width + width), F32),
        *rims, weights, weights_end,
        flops=flops(rows, depth, width),
    )

    masks = tuple(sorted(last))
    ends = [h for m in masks for h in last[m]]
    own_bc = run(
        functools.partial(last_bc, masks),
        ((rows, bc_width), BF16),
        *ends, weights_end, sums, rim_sums, conv_bc, bias_bc,
        scratch=[pltpu.VMEM((rows + RIM, bc_width), F32)],
        flops=flops(rows, depth, bc_width),
    )
    other_bc = partner(own_bc, "tp", 1)
    x, weighted = run(
        functools.partial(last_x, masks),
        [((rows, width), BF16), ((rows, width), BF16)],
        *ends, weights_end, sums, rim_sums, conv_x, bias_x, end_weight,
        scratch=[pltpu.VMEM((rows + RIM, width), F32)],
        flops=flops(rows, depth, width),
    )
    message_shape = ((n + 2 * PAD, width // 2), BF16)
    state_shape = (n, width // 2)
    message, kept = run(
        section_state,
        [message_shape, (state_shape, F32)],
        own_bc, other_bc, weighted, whole,
        flops=flops(rows, n, width),
    )
    received = partner(message, "ctx", 1)
    message = run(chip_state, message_shape, kept, whole, received)
    got = []
    for mask in range(1, chips):
        got.append(across_chips(message, mask))
    within = run(
        within_section,
        ((rows, width), F32),
        own_bc, other_bc, x, segment, skip_wide, message,
        flops=3 * flops(rows, rows, width),
    )
    gate = run(
        functools.partial(last_z, masks),
        ((rows, width), F32),
        *ends, weights_end, sums, message,
        flops=flops(rows, depth, width),
    )
    keep, give = run(
        entering_state, [(state_shape, BF16), (state_shape, BF16)], kept, whole, received, *got, within, gate
    )
    take = partner(give, "ctx", 1)
    half = width // 2
    mine, squares = run(
        gated_mine,
        [((rows, half), F32), ((rows, 128), F32)],
        own_bc, other_bc, keep, within, grown, gate,
        flops=flops(rows, n, half),
    )
    other, square = run(
        gated_other,
        [((rows, half), F32), ((ROWS, rows), F32)],
        own_bc, other_bc, take, within, grown, gate, squares,
        flops=flops(rows, n, half),
    )
    other_square = partner(square, "tp", 1)
    return run(
        normed_output,
        ((rows, width), BF16),
        mine, other, square, other_square, gain,
        scratch=[pltpu.VMEM((rows, width), BF16), pltpu.SemaphoreType.DMA((CHUNKS,))],
        out=HBM,
    )


def solution(mesh):
    in_specs = (
        P("ctx", "tp"),
        P(None, "tp"),
        P(None, "tp"),
        P(None, "tp"),
        P(None, "tp"),
        P(None, "tp"),
        P("tp"),
        P("tp"),
        P("ctx", "tp"),
        P("tp"),
        P("tp"),
        P("tp"),
    )
    out_specs = P("ctx", "tp")
    return jax.shard_map(local, mesh=mesh, in_specs=in_specs, out_specs=out_specs, check_vma=False)
```

```python
import functools

import jax
import jax.numpy as jnp
from jax import lax
from jax.experimental import pallas as pl
from jax.experimental.pallas import tpu as pltpu
from jax.sharding import PartitionSpec as P


KERNEL = 4
UPPER = 9
RIM = 8
ROWS = 8
CHUNKS = 4
TAIL = 8
F32, BF16 = jnp.float32, jnp.bfloat16
EXACT = lax.Precision.HIGHEST
VMEM = pl.BlockSpec(memory_space=pltpu.VMEM)
HBM = pl.BlockSpec(memory_space=pltpu.HBM)


def run(body, outs, *operands, scratch=(), flops=1000000, hbm=0, out=VMEM, limit=4 << 20):
    single = not isinstance(outs, list)
    shapes = [jax.ShapeDtypeStruct(*o) for o in ([outs] if single else outs)]
    operands = [
        pltpu.with_memory_space_constraint(o, pltpu.HBM) if i < hbm else o
        for i, o in enumerate(operands)
    ]
    call = pl.pallas_call(
        body,
        out_shape=shapes,
        in_specs=[HBM] * hbm + [VMEM] * (len(operands) - hbm),
        out_specs=[out] * len(shapes),
        scratch_shapes=list(scratch),
        compiler_params=pltpu.CompilerParams(vmem_limit_bytes=limit),
        cost_estimate=pl.CostEstimate(flops=flops, bytes_accessed=flops // 400, transcendentals=0),
    )
    results = call(*operands)
    return results[0] if single else results


def partner(value, axis, mask):
    return lax.ppermute(value, axis, [(i, i ^ mask) for i in range(lax.axis_size(axis))])


def across_chips(value, mask):
    return partner(value, "ctx", 2 * mask)


def onward(value, axis):
    size = lax.axis_size(axis)
    return lax.ppermute(value, axis, [(i, (i + 1) % size) for i in range(size)])


def dot(a, b, **kwargs):
    return jnp.dot(a, b, preferred_element_type=F32, **kwargs)


def two_parts(value):
    high = value.astype(BF16)
    return high, (value - high.astype(F32)).astype(BF16)


def silu(v):
    return v / (1.0 + jnp.exp(-v))


def holds_b():
    return lax.axis_index("tp") % 2 == 0


def first_core():
    return lax.axis_index("ctx") % 2 == 0


def whole_copies(sources, targets, arrivals, first):
    copies = [
        pltpu.make_async_copy(source, target, arrivals.at[first + i])
        for i, (source, target) in enumerate(zip(sources, targets))
    ]
    for copy in copies:
        copy.start()
    return copies


def fetched_halves(source, top, bottom, rim, tail, arrivals):
    rows = source.shape[0]
    copies = [
        pltpu.make_async_copy(source.at[pl.ds(start, out.shape[0])], out, arrivals.at[i])
        for i, (start, out) in enumerate(((top.shape[0], bottom), (0, top), (rows - RIM, tail)))
    ]
    for copy in copies:
        copy.start()
    for copy in copies:
        copy.wait()
    half = tail.shape[1] // 2
    last = tail[...].astype(F32)[RIM // 2 :]
    rim[...] = jnp.concatenate([last[:, :half], last[:, half:]], axis=0).astype(BF16)


def weight_copies(sources, weights, arrivals, masks):
    depth = weights.shape[1]
    copies = []
    for slot, mask in enumerate(masks):
        start = pl.multiple_of(jnp.bitwise_xor(lax.axis_index("tp"), mask) * depth, depth)
        column = 0
        for i, w in enumerate(sources):
            there = weights.at[slot, :, pl.ds(column, w.shape[1])]
            copies.append(
                pltpu.make_async_copy(w.at[pl.ds(start, depth)], there, arrivals.at[slot, i])
            )
            column += w.shape[1]
    for copy in copies:
        copy.start()
    return copies


def last_weights(masks, w_bc, w_x, w_z, *refs):
    count = (len(refs) - 3) // 2
    small, (weights, *held, arrivals, small_arrivals) = refs[:count], refs[count:]
    copies = weight_copies((w_bc, w_x, w_z), weights, arrivals, masks)
    for copy in copies + whole_copies(small, held, small_arrivals, 0):
        copy.wait()


def own_product(masks, w_bc, w_x, w_z, top, bottom, sums, weights, arrivals):
    copies = weight_copies((w_bc, w_x, w_z), weights, arrivals, masks)
    for copy in copies[:3]:
        copy.wait()
    sums[...] = dot(jnp.concatenate([top[...], bottom[...]], axis=0), weights[0])
    for copy in copies[3:]:
        copy.wait()


def block_of(pieces, i):
    return jnp.concatenate([pieces[2 * i][...], pieces[2 * i + 1][...]], axis=0)


def middle_product(masks, *refs):
    pieces, (weights, before, out) = refs[: 2 * len(masks)], refs[2 * len(masks) :]
    total = before[...]
    for i, mask in enumerate(masks):
        total += dot(block_of(pieces, i), weights[mask])
    out[...] = total


def rim_product(*refs):
    pieces, (early, last, out) = refs[:-3], refs[-3:]
    columns = pl.ds(0, out.shape[1])
    total = None
    for mask, piece in enumerate(pieces):
        count = early.shape[0]
        weights, slot = (early, mask) if mask < count else (last, mask - count)
        half = piece.shape[1]
        for side in range(2):
            term = dot(piece[...], weights[slot, pl.ds(side * half, half), columns])
            term = term[side * RIM // 2 : (side + 1) * RIM // 2]
            total = term if total is None else total + term
    inside = lax.axis_index("ctx") > 0
    total = jnp.where(inside, total, 0.0).astype(BF16).astype(F32)
    out[...] = jnp.concatenate([jnp.zeros_like(total), total], axis=0)


def finished(masks, pieces, weights, before, start, width):
    columns = pl.ds(start, width)
    total = before[:, columns]
    for i in range(len(masks)):
        total += dot(block_of(pieces, i), weights[i, :, columns])
    return total.astype(BF16).astype(F32)


def convolved(pre, rim, taps, bias, extended):
    rows = pre.shape[0]
    extended[pl.ds(0, RIM), :] = rim
    extended[pl.ds(RIM, rows), :] = pre
    total = bias[...]
    for k in range(KERNEL):
        total = total + taps[pl.ds(k, 1), :] * extended[pl.ds(RIM - KERNEL + 1 + k, rows), :]
    return silu(total).astype(BF16)


def last_bc(masks, *refs):
    pieces, refs = refs[: 2 * len(masks)], refs[2 * len(masks) :]
    weights, before, rim, taps, bias, out, extended = refs
    width = out.shape[1]
    pre = finished(masks, pieces, weights, before, 0, width)
    out[...] = convolved(pre, rim[:, pl.ds(0, width)], taps, bias, extended)


def last_x(masks, *refs):
    pieces, refs = refs[: 2 * len(masks)], refs[2 * len(masks) :]
    weights, before, rim, taps, bias, end_weight, x_out, weighted_out, extended = refs
    width = x_out.shape[1]
    start = rim.shape[1] - width
    pre = finished(masks, pieces, weights, before, start, width)
    x = convolved(pre, rim[:, pl.ds(start, width)], taps, bias, extended)
    x_out[...] = x
    weighted_out[...] = (x.astype(F32) * end_weight[...]).astype(BF16)


def last_z(masks, *refs):
    pieces, (weights, before, _, out) = refs[: 2 * len(masks)], refs[2 * len(masks) :]
    width = out.shape[1]
    out[...] = silu(finished(masks, pieces, weights, before, before.shape[1] - width, width))


def decays(decay_t, step, skip, segment, grown, end_weight, whole, skip_wide):
    heads, rows = decay_t.shape
    width = grown.shape[1]
    dim = width // heads
    spread = (
        lax.broadcasted_iota(jnp.int32, (heads, width), 1) // dim
        == lax.broadcasted_iota(jnp.int32, (heads, width), 0)
    ).astype(F32)
    i = lax.broadcasted_iota(jnp.int32, (rows, rows), 0)
    j = lax.broadcasted_iota(jnp.int32, (rows, rows), 1)
    causal = i >= j
    cum = lax.dot_general(
        causal.astype(F32),
        decay_t[...],
        (((1,), (1,)), ((), ())),
        precision=EXACT,
        preferred_element_type=F32,
    )
    cum_t = dot(decay_t[...], (i <= j).astype(F32), precision=EXACT)
    cum_wide = dot(cum, spread, precision=EXACT)
    total = cum_wide[rows - 1 :]
    grown[...] = jnp.exp(cum_wide)
    end_weight[...] = jnp.exp(total - cum_wide) * dot(step[...], spread, precision=EXACT)
    whole[...] = jnp.broadcast_to(jnp.exp(total), whole.shape)
    skip_wide[...] = dot(skip[...], spread, precision=EXACT)
    for h in range(heads):
        difference = cum[:, h : h + 1] - cum_t[h : h + 1, :]
        factor = jnp.where(causal, jnp.exp(jnp.where(causal, difference, 0.0)), 0.0)
        segment[h] = (factor * step[:, h : h + 1]).astype(BF16)


def halves(wide):
    half = wide.shape[1] // 2
    return wide[:, :half], wide[:, half:]


def mine_other(wide):
    low, high = halves(wide)
    first = first_core()
    return jnp.where(first, low, high), jnp.where(first, high, low)


def write_message(out, state, decay):
    n, width = state.shape
    tail = []
    for block in range(width // 128):
        columns = slice(block * 128, (block + 1) * 128)
        out[pl.ds(block * n, n), :] = state[:, columns].astype(BF16)
        high = decay[:, columns].astype(BF16).astype(F32)
        tail += [high, decay[:, columns] - high]
    rest = TAIL - len(tail)
    if rest:
        tail.append(jnp.zeros((rest, 128), F32))
    out[pl.ds(out.shape[0] - TAIL, TAIL), :] = jnp.concatenate(tail, axis=0).astype(BF16)


def read_message(ref, n):
    blocks = (ref.shape[0] - TAIL) // n
    tail = ref[pl.ds(blocks * n, TAIL), :].astype(F32)
    state = jnp.concatenate([ref[pl.ds(b * n, n), :] for b in range(blocks)], axis=1)
    decay = [tail[2 * b : 2 * b + 1] + tail[2 * b + 1 : 2 * b + 2] for b in range(blocks)]
    return state.astype(F32), jnp.concatenate(decay, axis=1)


def section_state(own_bc, other_bc, weighted, whole, message, kept):
    b = jnp.where(holds_b(), own_bc[...], other_bc[...])
    state = lax.dot_general(
        b, weighted[...], (((0,), (0,)), ((), ())), preferred_element_type=F32
    )
    mine, other = mine_other(state)
    _, other_decay = mine_other(whole[...])
    kept[...] = mine
    write_message(message, other, other_decay[:1])


def pair_states(kept, whole, received):
    sibling, sibling_decay = read_message(received, kept.shape[0])
    mine_decay, _ = mine_other(whole[...])
    mine_decay = mine_decay[:1]
    first = first_core()
    mine = kept[...]
    return (
        (jnp.where(first, mine, sibling), jnp.where(first, mine_decay, sibling_decay)),
        (jnp.where(first, sibling, mine), jnp.where(first, sibling_decay, mine_decay)),
    )


def chip_state(kept, whole, received, message):
    (first, first_decay), (second, second_decay) = pair_states(kept, whole, received)
    write_message(message, second + second_decay * first, first_decay * second_decay)


def entering_state(kept, whole, received, *refs):
    got, (_, _, keep, give) = refs[:-4], refs[-4:]
    (first, first_decay), _ = pair_states(kept, whole, received)
    chip = lax.axis_index("ctx") // 2
    messages = [read_message(ref, kept.shape[0]) for ref in got]
    places = [jnp.bitwise_xor(chip, mask) for mask in range(1, len(got) + 1)]
    before = jnp.zeros_like(first)
    for place, (state, _) in zip(places, messages):
        weight = jnp.ones_like(first_decay)
        for other, (_, decay) in zip(places, messages):
            weight *= jnp.where((other > place) & (other < chip), decay, 1.0)
        before += jnp.where(place < chip, weight, 0.0) * state
    after = first + first_decay * before
    lead = first_core()
    keep[...] = jnp.where(lead, before, after).astype(BF16)
    give[...] = jnp.where(lead, after, before).astype(BF16)


def within_section(own_bc, other_bc, x, segment, skip_wide, _, out):
    own, other = own_bc[...], other_bc[...]
    b = jnp.where(holds_b(), own, other)
    c = jnp.where(holds_b(), other, own)
    scores = lax.dot_general(c, b, (((1,), (1,)), ((), ())), preferred_element_type=F32)
    heads = segment.shape[0]
    dim = x.shape[1] // heads
    low = lax.broadcasted_iota(jnp.int32, (1, 2 * dim), 1) < dim
    for pair in range(heads // 2):
        columns = pl.ds(pair * 2 * dim, 2 * dim)
        mixing = jnp.concatenate(
            [(segment[2 * pair + s].astype(F32) * scores).astype(BF16) for s in range(2)], axis=1
        )
        both = x[:, columns]
        wide = both.astype(F32)
        stacked = jnp.concatenate(
            [jnp.where(low, wide, 0.0).astype(BF16), jnp.where(low, 0.0, wide).astype(BF16)], axis=0
        )
        out[:, columns] = dot(mixing, stacked) + skip_wide[:, columns] * wide


def gated_half(c, state, start, within, grown, gate):
    half = state.shape[1]
    columns = pl.ds(start, half)
    gated = (within[:, columns] + dot(c, state) * grown[:, columns]) * gate[:, columns]
    squares = None
    for lane in range(0, half, 128):
        part = gated[:, lane : lane + 128]
        squares = part * part if squares is None else squares + part * part
    return gated, squares


def half_starts(half):
    core = lax.axis_index("ctx") % 2
    return [pl.multiple_of(place * half, 128) for place in (core, 1 - core)]


def gated_mine(own_bc, other_bc, keep, within, grown, gate, gated_out, squares_out):
    c = jnp.where(holds_b(), other_bc[...], own_bc[...])
    mine, _ = half_starts(keep.shape[1])
    gated_out[...], squares_out[...] = gated_half(c, keep[...], mine, within, grown, gate)


def gated_other(own_bc, other_bc, take, within, grown, gate, squares, gated_out, square_out):
    c = jnp.where(holds_b(), other_bc[...], own_bc[...])
    _, other = half_starts(take.shape[1])
    gated_out[...], more = gated_half(c, take[...], other, within, grown, gate)
    ones = jnp.ones((ROWS, more.shape[1]), BF16)
    square_out[...] = sum(
        lax.dot_general(ones, part, (((1,), (1,)), ((), ())), preferred_element_type=F32)
        for part in two_parts(squares[...] + more)
    )


def normed_output(mine, other, square, other_square, gain, out, held, sent):
    rows, half = mine.shape
    mean = (square[...] + other_square[...]) / (4 * half)
    share = jnp.full((ROWS, 128), 1.0 / ROWS, BF16)
    factor = sum(
        lax.dot_general(part, share, (((0,), (0,)), ((), ())), preferred_element_type=F32)
        for part in two_parts(lax.rsqrt(mean + 1e-05))
    )
    copies = []
    count = rows // CHUNKS
    for chunk in range(CHUNKS):
        some = pl.ds(chunk * count, count)
        column = factor[chunk * count : (chunk + 1) * count]
        for gated, start in zip((mine, other), half_starts(half)):
            for lane in range(0, half, 128):
                columns = pl.ds(pl.multiple_of(start + lane, 128), 128)
                wide = gated[some, pl.ds(lane, 128)] * column * gain[:, columns]
                held[some, columns] = wide.astype(BF16)
        copies.append(pltpu.make_async_copy(held.at[some], out.at[some], sent.at[chunk]))
        copies[-1].start()
    for copy in copies:
        copy.wait()


def gather_pieces(top, bottom, axis):
    size = lax.axis_size(axis)
    near_bottom = partner(bottom, axis, 1)
    far_top = partner(top, axis, 2)
    near_top = partner(top, axis, 1)
    far_bottom = partner(bottom, axis, 2)
    across_bottom = partner(near_bottom, axis, 2)
    across_top = partner(far_top, axis, 1)
    early = {1: [near_top, near_bottom], 2: [far_top, far_bottom]}
    last = {3: [across_top, across_bottom]}
    mask = 4
    while mask < size:
        early = {**early, **last}
        last = {m | mask: [partner(h, axis, mask) for h in p] for m, p in early.items()}
        last[mask] = [partner(h, axis, mask) for h in (top, bottom)]
        mask *= 2
    return early, last


def gather_rim(rim, axis):
    pieces = [onward(rim, "ctx")]
    for mask in range(1, lax.axis_size(axis)):
        pieces.append(partner(pieces[0], axis, mask))
    return pieces


def local(
    tokens, w_z, w_x, w_bc, conv_x, conv_bc, bias_x, bias_bc, decay_logarithm, head_step, skip, gain
):
    rows, depth = tokens.shape
    width, bc_width = w_x.shape[1], w_bc.shape[1]
    heads = head_step.shape[0]
    n = bc_width
    chips = lax.axis_size("ctx") // 2

    upper = rows * UPPER // 16
    top, bottom, rim = run(
        fetched_halves,
        [((upper, depth), BF16), ((rows - upper, depth), BF16), ((RIM, depth // 2), BF16)],
        tokens,
        scratch=[pltpu.VMEM((RIM, depth), BF16), pltpu.SemaphoreType.DMA((3,))],
        hbm=1,
    )

    def flops(*sizes):
        total = 2
        for s in sizes:
            total *= s
        return total

    early, last = gather_pieces(top, bottom, "tp")
    rims = gather_rim(rim, "tp")
    everything = bc_width + 2 * width
    masks = (0, *sorted(early))
    sums, weights = run(
        functools.partial(own_product, masks),
        [((rows, everything), F32), ((len(masks), depth, everything), BF16)],
        w_bc, w_x, w_z, top, bottom,
        scratch=[pltpu.SemaphoreType.DMA((len(masks), 3))],
        flops=flops(rows, depth, everything),
        hbm=3,
    )
    masks = tuple(sorted(last))
    vectors = [conv_bc, bias_bc, conv_x, bias_x, gain, decay_logarithm.T, head_step, skip]
    vectors = [v if v.ndim == 2 else v.reshape(1, -1) for v in vectors]
    weights_end, conv_bc, bias_bc, conv_x, bias_x, gain, *small = run(
        functools.partial(last_weights, masks),
        [((len(masks), depth, everything), BF16), *[(v.shape, F32) for v in vectors]],
        w_bc, w_x, w_z, *vectors,
        scratch=[
            pltpu.SemaphoreType.DMA((len(masks), 3)),
            pltpu.SemaphoreType.DMA((len(vectors),)),
        ],
        hbm=3 + len(vectors),
    )
    segment, grown, end_weight, whole, skip_wide = run(
        decays,
        [
            ((heads, rows, rows), BF16),
            ((rows, width), F32),
            ((rows, width), F32),
            ((ROWS, width), F32),
            ((1, width), F32),
        ],
        *small,
        flops=flops(rows, rows, width),
    )
    masks = tuple(sorted(early))
    sums = run(
        functools.partial(middle_product, masks),
        ((rows, everything), F32),
        *[h for m in masks for h in early[m]], weights, sums,
        flops=len(masks) * flops(rows, depth, everything),
    )
    rim_sums = run(
        rim_product,
        ((RIM, bc_width + width), F32),
        *rims, weights, weights_end,
        flops=flops(rows, depth, width),
    )

    masks = tuple(sorted(last))
    ends = [h for m in masks for h in last[m]]
    own_bc = run(
        functools.partial(last_bc, masks),
        ((rows, bc_width), BF16),
        *ends, weights_end, sums, rim_sums, conv_bc, bias_bc,
        scratch=[pltpu.VMEM((rows + RIM, bc_width), F32)],
        flops=flops(rows, depth, bc_width),
    )
    other_bc = partner(own_bc, "tp", 1)
    x, weighted = run(
        functools.partial(last_x, masks),
        [((rows, width), BF16), ((rows, width), BF16)],
        *ends, weights_end, sums, rim_sums, conv_x, bias_x, end_weight,
        scratch=[pltpu.VMEM((rows + RIM, width), F32)],
        flops=flops(rows, depth, width),
    )
    message_shape = ((n * width // 256 + TAIL, 128), BF16)
    state_shape = (n, width // 2)
    message, kept = run(
        section_state,
        [message_shape, (state_shape, F32)],
        own_bc, other_bc, weighted, whole,
        flops=flops(rows, n, width),
    )
    received = partner(message, "ctx", 1)
    message = run(chip_state, message_shape, kept, whole, received)
    got = []
    for mask in range(1, chips):
        got.append(across_chips(message, mask))
    within = run(
        within_section,
        ((rows, width), F32),
        own_bc, other_bc, x, segment, skip_wide, message,
        flops=3 * flops(rows, rows, width),
    )
    gate = run(
        functools.partial(last_z, masks),
        ((rows, width), F32),
        *ends, weights_end, sums, message,
        flops=flops(rows, depth, width),
    )
    keep, give = run(
        entering_state, [(state_shape, BF16), (state_shape, BF16)], kept, whole, received, *got, within, gate
    )
    take = partner(give, "ctx", 1)
    half = width // 2
    mine, squares = run(
        gated_mine,
        [((rows, half), F32), ((rows, 128), F32)],
        own_bc, other_bc, keep, within, grown, gate,
        flops=flops(rows, n, half),
    )
    other, square = run(
        gated_other,
        [((rows, half), F32), ((ROWS, rows), F32)],
        own_bc, other_bc, take, within, grown, gate, squares,
        flops=flops(rows, n, half),
    )
    other_square = partner(square, "tp", 1)
    return run(
        normed_output,
        ((rows, width), BF16),
        mine, other, square, other_square, gain,
        scratch=[pltpu.VMEM((rows, width), BF16), pltpu.SemaphoreType.DMA((CHUNKS,))],
        out=HBM,
    )


def solution(mesh):
    in_specs = (
        P("ctx", "tp"),
        P(None, "tp"),
        P(None, "tp"),
        P(None, "tp"),
        P(None, "tp"),
        P(None, "tp"),
        P("tp"),
        P("tp"),
        P("ctx", "tp"),
        P("tp"),
        P("tp"),
        P("tp"),
    )
    out_specs = P("ctx", "tp")
    return jax.shard_map(local, mesh=mesh, in_specs=in_specs, out_specs=out_specs, check_vma=False)
```

```python
import functools

import jax
import jax.numpy as jnp
from jax import lax
from jax.experimental import pallas as pl
from jax.experimental.pallas import tpu as pltpu
from jax.sharding import PartitionSpec as P


KERNEL = 4
UPPER = 9
RIM = 8
ROWS = 8
CHUNKS = 4
TAIL = 8
F32, BF16 = jnp.float32, jnp.bfloat16
EXACT = lax.Precision.HIGHEST
VMEM = pl.BlockSpec(memory_space=pltpu.VMEM)
HBM = pl.BlockSpec(memory_space=pltpu.HBM)


def run(body, outs, *operands, scratch=(), flops=1000000, hbm=0, out=VMEM, limit=4 << 20):
    single = not isinstance(outs, list)
    shapes = [jax.ShapeDtypeStruct(*o) for o in ([outs] if single else outs)]
    operands = [
        pltpu.with_memory_space_constraint(o, pltpu.HBM) if i < hbm else o
        for i, o in enumerate(operands)
    ]
    call = pl.pallas_call(
        body,
        out_shape=shapes,
        in_specs=[HBM] * hbm + [VMEM] * (len(operands) - hbm),
        out_specs=[out] * len(shapes),
        scratch_shapes=list(scratch),
        compiler_params=pltpu.CompilerParams(vmem_limit_bytes=limit),
        cost_estimate=pl.CostEstimate(flops=flops, bytes_accessed=flops // 400, transcendentals=0),
    )
    results = call(*operands)
    return results[0] if single else results


def partner(value, axis, mask):
    return lax.ppermute(value, axis, [(i, i ^ mask) for i in range(lax.axis_size(axis))])


def across_chips(value, mask):
    return partner(value, "ctx", 2 * mask)


def onward(value, axis):
    size = lax.axis_size(axis)
    return lax.ppermute(value, axis, [(i, (i + 1) % size) for i in range(size)])


def dot(a, b, **kwargs):
    return jnp.dot(a, b, preferred_element_type=F32, **kwargs)


def two_parts(value):
    high = value.astype(BF16)
    return high, (value - high.astype(F32)).astype(BF16)


def silu(v):
    return v / (1.0 + jnp.exp(-v))


def holds_b():
    return lax.axis_index("tp") % 2 == 0


def first_core():
    return lax.axis_index("ctx") % 2 == 0


def whole_copies(sources, targets, arrivals, first):
    copies = [
        pltpu.make_async_copy(source, target, arrivals.at[first + i])
        for i, (source, target) in enumerate(zip(sources, targets))
    ]
    for copy in copies:
        copy.start()
    return copies


def fetched_halves(source, top, bottom, rim, tail, arrivals):
    rows = source.shape[0]
    copies = [
        pltpu.make_async_copy(source.at[pl.ds(start, out.shape[0])], out, arrivals.at[i])
        for i, (start, out) in enumerate(((top.shape[0], bottom), (0, top), (rows - RIM, tail)))
    ]
    for copy in copies:
        copy.start()
    for copy in copies:
        copy.wait()
    half = tail.shape[1] // 2
    last = tail[...].astype(F32)[RIM // 2 :]
    rim[...] = jnp.concatenate([last[:, :half], last[:, half:]], axis=0).astype(BF16)


def weight_copies(sources, weights, arrivals, masks):
    depth = weights.shape[1]
    copies = []
    for slot, mask in enumerate(masks):
        start = pl.multiple_of(jnp.bitwise_xor(lax.axis_index("tp"), mask) * depth, depth)
        column = 0
        for i, w in enumerate(sources):
            there = weights.at[slot, :, pl.ds(column, w.shape[1])]
            copies.append(
                pltpu.make_async_copy(w.at[pl.ds(start, depth)], there, arrivals.at[slot, i])
            )
            column += w.shape[1]
    for copy in copies:
        copy.start()
    return copies


def last_weights(masks, w_bc, w_x, w_z, *refs):
    count = (len(refs) - 3) // 2
    small, (weights, *held, arrivals, small_arrivals) = refs[:count], refs[count:]
    copies = weight_copies((w_bc, w_x, w_z), weights, arrivals, masks)
    for copy in copies + whole_copies(small, held, small_arrivals, 0):
        copy.wait()


def with_rim(parts, rim):
    wide = rim[...].astype(F32)
    half = RIM // 2
    last = jnp.concatenate([wide[:half], wide[half:]], axis=1)
    tail = jnp.concatenate([jnp.zeros_like(last), last], axis=0).astype(BF16)
    return jnp.concatenate([part[...] for part in parts] + [tail], axis=0)


def own_product(masks, w_bc, w_x, w_z, top, bottom, rim, sums, weights, arrivals):
    copies = weight_copies((w_bc, w_x, w_z), weights, arrivals, masks)
    for copy in copies[:3]:
        copy.wait()
    sums[...] = dot(with_rim((top, bottom), rim), weights[0])
    for copy in copies[3:]:
        copy.wait()


def middle_product(masks, *refs):
    count = 3 * len(masks)
    pieces, (weights, before, out) = refs[:count], refs[count:]
    total = before[...]
    for i, mask in enumerate(masks):
        total += dot(with_rim(pieces[3 * i : 3 * i + 2], pieces[3 * i + 2]), weights[mask])
    out[...] = total


def finished(masks, pieces, weights, before, start, width):
    columns = pl.ds(start, width)
    total = before[:, columns]
    for i in range(len(masks)):
        block = with_rim(pieces[3 * i : 3 * i + 2], pieces[3 * i + 2])
        total += dot(block, weights[i, :, columns])
    total = total.astype(BF16).astype(F32)
    rows = total.shape[0] - RIM
    inside = lax.axis_index("ctx") > 0
    return total[:rows], jnp.where(inside, total[rows:], 0.0)


def convolved(pre, rim, taps, bias, extended):
    rows = pre.shape[0]
    extended[pl.ds(0, RIM), :] = rim
    extended[pl.ds(RIM, rows), :] = pre
    total = bias[...]
    for k in range(KERNEL):
        total = total + taps[pl.ds(k, 1), :] * extended[pl.ds(RIM - KERNEL + 1 + k, rows), :]
    return silu(total).astype(BF16)


def last_bc(masks, *refs):
    count = 3 * len(masks)
    pieces, (weights, before, taps, bias, out, extended) = refs[:count], refs[count:]
    pre, rim = finished(masks, pieces, weights, before, 0, out.shape[1])
    out[...] = convolved(pre, rim, taps, bias, extended)


def last_x(masks, *refs):
    count = 3 * len(masks)
    pieces, refs = refs[:count], refs[count:]
    weights, before, taps, bias, end_weight, x_out, weighted_out, extended = refs
    width = x_out.shape[1]
    start = before.shape[1] - 2 * width
    pre, rim = finished(masks, pieces, weights, before, start, width)
    x = convolved(pre, rim, taps, bias, extended)
    x_out[...] = x
    weighted_out[...] = (x.astype(F32) * end_weight[...]).astype(BF16)


def last_z(masks, *refs):
    count = 3 * len(masks)
    pieces, (weights, before, _, out) = refs[:count], refs[count:]
    width = out.shape[1]
    pre, _ = finished(masks, pieces, weights, before, before.shape[1] - width, width)
    out[...] = silu(pre)


def decays(decay_t, step, skip, segment, grown, end_weight, whole, skip_wide):
    heads, rows = decay_t.shape
    width = grown.shape[1]
    dim = width // heads
    spread = (
        lax.broadcasted_iota(jnp.int32, (heads, width), 1) // dim
        == lax.broadcasted_iota(jnp.int32, (heads, width), 0)
    ).astype(F32)
    i = lax.broadcasted_iota(jnp.int32, (rows, rows), 0)
    j = lax.broadcasted_iota(jnp.int32, (rows, rows), 1)
    causal = i >= j
    cum = lax.dot_general(
        causal.astype(F32),
        decay_t[...],
        (((1,), (1,)), ((), ())),
        precision=EXACT,
        preferred_element_type=F32,
    )
    cum_t = dot(decay_t[...], (i <= j).astype(F32), precision=EXACT)
    cum_wide = dot(cum, spread, precision=EXACT)
    total = cum_wide[rows - 1 :]
    grown[...] = jnp.exp(cum_wide)
    end_weight[...] = jnp.exp(total - cum_wide) * dot(step[...], spread, precision=EXACT)
    whole[...] = jnp.broadcast_to(jnp.exp(total), whole.shape)
    skip_wide[...] = dot(skip[...], spread, precision=EXACT)
    for h in range(heads):
        difference = cum[:, h : h + 1] - cum_t[h : h + 1, :]
        factor = jnp.where(causal, jnp.exp(jnp.where(causal, difference, 0.0)), 0.0)
        segment[h] = (factor * step[:, h : h + 1]).astype(BF16)


def halves(wide):
    half = wide.shape[1] // 2
    return wide[:, :half], wide[:, half:]


def mine_other(wide):
    low, high = halves(wide)
    first = first_core()
    return jnp.where(first, low, high), jnp.where(first, high, low)


def write_message(out, state, decay):
    n, width = state.shape
    tail = []
    for block in range(width // 128):
        columns = slice(block * 128, (block + 1) * 128)
        out[pl.ds(block * n, n), :] = state[:, columns].astype(BF16)
        high = decay[:, columns].astype(BF16).astype(F32)
        tail += [high, decay[:, columns] - high]
    rest = TAIL - len(tail)
    if rest:
        tail.append(jnp.zeros((rest, 128), F32))
    out[pl.ds(out.shape[0] - TAIL, TAIL), :] = jnp.concatenate(tail, axis=0).astype(BF16)


def read_message(ref, n):
    blocks = (ref.shape[0] - TAIL) // n
    tail = ref[pl.ds(blocks * n, TAIL), :].astype(F32)
    state = jnp.concatenate([ref[pl.ds(b * n, n), :] for b in range(blocks)], axis=1)
    decay = [tail[2 * b : 2 * b + 1] + tail[2 * b + 1 : 2 * b + 2] for b in range(blocks)]
    return state.astype(F32), jnp.concatenate(decay, axis=1)


def section_state(own_bc, other_bc, weighted, whole, message, kept):
    b = jnp.where(holds_b(), own_bc[...], other_bc[...])
    state = lax.dot_general(
        b, weighted[...], (((0,), (0,)), ((), ())), preferred_element_type=F32
    )
    mine, other = mine_other(state)
    _, other_decay = mine_other(whole[...])
    kept[...] = mine
    write_message(message, other, other_decay[:1])


def pair_states(kept, whole, received):
    sibling, sibling_decay = read_message(received, kept.shape[0])
    mine_decay, _ = mine_other(whole[...])
    mine_decay = mine_decay[:1]
    first = first_core()
    mine = kept[...]
    return (
        (jnp.where(first, mine, sibling), jnp.where(first, mine_decay, sibling_decay)),
        (jnp.where(first, sibling, mine), jnp.where(first, sibling_decay, mine_decay)),
    )


def chip_state(kept, whole, received, message):
    (first, first_decay), (second, second_decay) = pair_states(kept, whole, received)
    write_message(message, second + second_decay * first, first_decay * second_decay)


def entering_state(kept, whole, received, *refs):
    got, (_, _, keep, give) = refs[:-4], refs[-4:]
    (first, first_decay), _ = pair_states(kept, whole, received)
    chip = lax.axis_index("ctx") // 2
    messages = [read_message(ref, kept.shape[0]) for ref in got]
    places = [jnp.bitwise_xor(chip, mask) for mask in range(1, len(got) + 1)]
    before = jnp.zeros_like(first)
    for place, (state, _) in zip(places, messages):
        weight = jnp.ones_like(first_decay)
        for other, (_, decay) in zip(places, messages):
            weight *= jnp.where((other > place) & (other < chip), decay, 1.0)
        before += jnp.where(place < chip, weight, 0.0) * state
    after = first + first_decay * before
    lead = first_core()
    keep[...] = jnp.where(lead, before, after).astype(BF16)
    give[...] = jnp.where(lead, after, before).astype(BF16)


def within_section(own_bc, other_bc, x, segment, skip_wide, _, out):
    own, other = own_bc[...], other_bc[...]
    b = jnp.where(holds_b(), own, other)
    c = jnp.where(holds_b(), other, own)
    scores = lax.dot_general(c, b, (((1,), (1,)), ((), ())), preferred_element_type=F32)
    heads = segment.shape[0]
    dim = x.shape[1] // heads
    low = lax.broadcasted_iota(jnp.int32, (1, 2 * dim), 1) < dim
    for pair in range(heads // 2):
        columns = pl.ds(pair * 2 * dim, 2 * dim)
        mixing = jnp.concatenate(
            [(segment[2 * pair + s].astype(F32) * scores).astype(BF16) for s in range(2)], axis=1
        )
        both = x[:, columns]
        wide = both.astype(F32)
        stacked = jnp.concatenate(
            [jnp.where(low, wide, 0.0).astype(BF16), jnp.where(low, 0.0, wide).astype(BF16)], axis=0
        )
        out[:, columns] = dot(mixing, stacked) + skip_wide[:, columns] * wide


def gated_half(c, state, start, within, grown, gate):
    half = state.shape[1]
    columns = pl.ds(start, half)
    gated = (within[:, columns] + dot(c, state) * grown[:, columns]) * gate[:, columns]
    squares = None
    for lane in range(0, half, 128):
        part = gated[:, lane : lane + 128]
        squares = part * part if squares is None else squares + part * part
    return gated, squares


def half_starts(half):
    core = lax.axis_index("ctx") % 2
    return [pl.multiple_of(place * half, 128) for place in (core, 1 - core)]


def gated_mine(own_bc, other_bc, keep, within, grown, gate, gated_out, squares_out):
    c = jnp.where(holds_b(), other_bc[...], own_bc[...])
    mine, _ = half_starts(keep.shape[1])
    gated_out[...], squares_out[...] = gated_half(c, keep[...], mine, within, grown, gate)


def gated_other(own_bc, other_bc, take, within, grown, gate, squares, gated_out, square_out):
    c = jnp.where(holds_b(), other_bc[...], own_bc[...])
    _, other = half_starts(take.shape[1])
    gated_out[...], more = gated_half(c, take[...], other, within, grown, gate)
    ones = jnp.ones((ROWS, more.shape[1]), BF16)
    square_out[...] = sum(
        lax.dot_general(ones, part, (((1,), (1,)), ((), ())), preferred_element_type=F32)
        for part in two_parts(squares[...] + more)
    )


def normed_output(mine, other, square, other_square, gain, out, held, sent):
    rows, half = mine.shape
    mean = (square[...] + other_square[...]) / (4 * half)
    share = jnp.full((ROWS, 128), 1.0 / ROWS, BF16)
    factor = sum(
        lax.dot_general(part, share, (((0,), (0,)), ((), ())), preferred_element_type=F32)
        for part in two_parts(lax.rsqrt(mean + 1e-05))
    )
    copies = []
    count = rows // CHUNKS
    for chunk in range(CHUNKS):
        some = pl.ds(chunk * count, count)
        column = factor[chunk * count : (chunk + 1) * count]
        for gated, start in zip((mine, other), half_starts(half)):
            for lane in range(0, half, 128):
                columns = pl.ds(pl.multiple_of(start + lane, 128), 128)
                wide = gated[some, pl.ds(lane, 128)] * column * gain[:, columns]
                held[some, columns] = wide.astype(BF16)
        copies.append(pltpu.make_async_copy(held.at[some], out.at[some], sent.at[chunk]))
        copies[-1].start()
    for copy in copies:
        copy.wait()


def gather_pieces(top, bottom, axis):
    size = lax.axis_size(axis)
    near_bottom = partner(bottom, axis, 1)
    far_top = partner(top, axis, 2)
    near_top = partner(top, axis, 1)
    far_bottom = partner(bottom, axis, 2)
    across_bottom = partner(near_bottom, axis, 2)
    across_top = partner(far_top, axis, 1)
    early = {1: [near_top, near_bottom], 2: [far_top, far_bottom]}
    last = {3: [across_top, across_bottom]}
    mask = 4
    while mask < size:
        early = {**early, **last}
        last = {m | mask: [partner(h, axis, mask) for h in p] for m, p in early.items()}
        last[mask] = [partner(h, axis, mask) for h in (top, bottom)]
        mask *= 2
    return early, last


def gather_rim(rim, axis):
    pieces = [onward(rim, "ctx")]
    for mask in range(1, lax.axis_size(axis)):
        pieces.append(partner(pieces[0], axis, mask))
    return pieces


def local(
    tokens, w_z, w_x, w_bc, conv_x, conv_bc, bias_x, bias_bc, decay_logarithm, head_step, skip, gain
):
    rows, depth = tokens.shape
    width, bc_width = w_x.shape[1], w_bc.shape[1]
    heads = head_step.shape[0]
    n = bc_width
    chips = lax.axis_size("ctx") // 2

    upper = rows * UPPER // 16
    top, bottom, rim = run(
        fetched_halves,
        [((upper, depth), BF16), ((rows - upper, depth), BF16), ((RIM, depth // 2), BF16)],
        tokens,
        scratch=[pltpu.VMEM((RIM, depth), BF16), pltpu.SemaphoreType.DMA((3,))],
        hbm=1,
    )

    def flops(*sizes):
        total = 2
        for s in sizes:
            total *= s
        return total

    early, last = gather_pieces(top, bottom, "tp")
    rims = gather_rim(rim, "tp")
    everything = bc_width + 2 * width
    masks = (0, *sorted(early))
    sums, weights = run(
        functools.partial(own_product, masks),
        [((rows + RIM, everything), F32), ((len(masks), depth, everything), BF16)],
        w_bc, w_x, w_z, top, bottom, rims[0],
        scratch=[pltpu.SemaphoreType.DMA((len(masks), 3))],
        flops=flops(rows, depth, everything),
        hbm=3,
    )
    masks = tuple(sorted(last))
    vectors = [conv_bc, bias_bc, conv_x, bias_x, gain, decay_logarithm.T, head_step, skip]
    vectors = [v if v.ndim == 2 else v.reshape(1, -1) for v in vectors]
    weights_end, conv_bc, bias_bc, conv_x, bias_x, gain, *small = run(
        functools.partial(last_weights, masks),
        [((len(masks), depth, everything), BF16), *[(v.shape, F32) for v in vectors]],
        w_bc, w_x, w_z, *vectors,
        scratch=[
            pltpu.SemaphoreType.DMA((len(masks), 3)),
            pltpu.SemaphoreType.DMA((len(vectors),)),
        ],
        hbm=3 + len(vectors),
    )
    segment, grown, end_weight, whole, skip_wide = run(
        decays,
        [
            ((heads, rows, rows), BF16),
            ((rows, width), F32),
            ((rows, width), F32),
            ((ROWS, width), F32),
            ((1, width), F32),
        ],
        *small,
        flops=flops(rows, rows, width),
    )
    masks = tuple(sorted(early))
    sums = run(
        functools.partial(middle_product, masks),
        ((rows + RIM, everything), F32),
        *[h for m in masks for h in (*early[m], rims[m])], weights, sums,
        flops=len(masks) * flops(rows, depth, everything),
    )
    masks = tuple(sorted(last))
    ends = [h for m in masks for h in (*last[m], rims[m])]
    own_bc = run(
        functools.partial(last_bc, masks),
        ((rows, bc_width), BF16),
        *ends, weights_end, sums, conv_bc, bias_bc,
        scratch=[pltpu.VMEM((rows + RIM, bc_width), F32)],
        flops=flops(rows, depth, bc_width),
    )
    other_bc = partner(own_bc, "tp", 1)
    x, weighted = run(
        functools.partial(last_x, masks),
        [((rows, width), BF16), ((rows, width), BF16)],
        *ends, weights_end, sums, conv_x, bias_x, end_weight,
        scratch=[pltpu.VMEM((rows + RIM, width), F32)],
        flops=flops(rows, depth, width),
    )
    message_shape = ((n * width // 256 + TAIL, 128), BF16)
    state_shape = (n, width // 2)
    message, kept = run(
        section_state,
        [message_shape, (state_shape, F32)],
        own_bc, other_bc, weighted, whole,
        flops=flops(rows, n, width),
    )
    received = partner(message, "ctx", 1)
    message = run(chip_state, message_shape, kept, whole, received)
    got = []
    for mask in range(1, chips):
        got.append(across_chips(message, mask))
    within = run(
        within_section,
        ((rows, width), F32),
        own_bc, other_bc, x, segment, skip_wide, message,
        flops=3 * flops(rows, rows, width),
    )
    gate = run(
        functools.partial(last_z, masks),
        ((rows, width), F32),
        *ends, weights_end, sums, message,
        flops=flops(rows, depth, width),
    )
    keep, give = run(
        entering_state, [(state_shape, BF16), (state_shape, BF16)], kept, whole, received, *got, within, gate
    )
    take = partner(give, "ctx", 1)
    half = width // 2
    mine, squares = run(
        gated_mine,
        [((rows, half), F32), ((rows, 128), F32)],
        own_bc, other_bc, keep, within, grown, gate,
        flops=flops(rows, n, half),
    )
    other, square = run(
        gated_other,
        [((rows, half), F32), ((ROWS, rows), F32)],
        own_bc, other_bc, take, within, grown, gate, squares,
        flops=flops(rows, n, half),
    )
    other_square = partner(square, "tp", 1)
    return run(
        normed_output,
        ((rows, width), BF16),
        mine, other, square, other_square, gain,
        scratch=[pltpu.VMEM((rows, width), BF16), pltpu.SemaphoreType.DMA((CHUNKS,))],
        out=HBM,
    )


def solution(mesh):
    in_specs = (
        P("ctx", "tp"),
        P(None, "tp"),
        P(None, "tp"),
        P(None, "tp"),
        P(None, "tp"),
        P(None, "tp"),
        P("tp"),
        P("tp"),
        P("ctx", "tp"),
        P("tp"),
        P("tp"),
        P("tp"),
    )
    out_specs = P("ctx", "tp")
    return jax.shard_map(local, mesh=mesh, in_specs=in_specs, out_specs=out_specs, check_vma=False)
```
